32 devices in a mesh: wide: 8 (over y, x, core), shard: 4 (over z).
Axes of the slice: x: 2, y: 2, z: 4, core: 2. Of those that a mesh axis runs over, the one named last changes fastest.
Arguments:
- tokens: bfloat16 [32768, 1152], P(('wide', 'shard')), may hold values from -6 to 6
- seg_ids: int32 [32768], P(('wide', 'shard')), may hold values from -1 to 63, as said below
- cotangent: bfloat16 [32768, 1152], P(('wide', 'shard')), may hold values from -6 to 6
- params: float32 [23296, 1152], P('shard'), may hold values from -6 to 6
- gains: float32 [4, 1152], P(None, 'shard'), may hold values from -0.06 to 0.06
- first_moment: float32 [23296, 1152], P('shard'), may hold values from -119.47276 to 119.47276
- second_moment: float32 [23296, 1152], P('shard'), may hold values from 1736.704 to 6881.28
- gain_first: float32 [4, 1152], P(None, 'shard'), may hold values from -119.47276 to 119.47276
- gain_second: float32 [4, 1152], P(None, 'shard'), may hold values from 1736.704 to 6881.28
Outputs:
- result: bfloat16 [32768, 1152], P(('wide', 'shard'))
- input_grad: bfloat16 [32768, 1152], P(('wide', 'shard'))
- row_grad: float32 [23296, 1152], P('shard')
- gain_grad: float32 [4, 1152], P(None, 'shard')
- new_params: float32 [23296, 1152], P('shard')
- new_gains: float32 [4, 1152], P(None, 'shard')
- new_first: float32 [23296, 1152], P('shard')
- new_second: float32 [23296, 1152], P('shard')
- new_gain_first: float32 [4, 1152], P(None, 'shard')
- new_gain_second: float32 [4, 1152], P(None, 'shard')
The draws below stay inside these ranges and needn't reach their ends.
Inputs may be any that keep to these rules, and one draw needn't show every extreme that they name: `seg_ids`: within each device's 1024 slots the ids start at 0, never fall, and each id covers consecutive slots of one sequence; -1 marks the empty slots at the end of a device; some device holds one sequence of 1024 tokens, some device has empty slots, and some device holds 64 sequences.
All inputs are finite; a program needn't handle non-finite values.
Results may differ from the reference program's by a relative error of at most 0.018.
The reference program's roundings to bfloat16 on the way count: a program that leaves them out, or rounds other values in their place, can miss the bound.
Values may be sent and summed in bfloat16 or wider, within the bound.
No kernel may reach another device: no remote copies, remote signals or barrier semaphores. Data moves between devices by JAX's collectives and lax.ppermute only.
A program may use at most 704 MiB of HBM per device.

```python
import math
import jax
import jax.numpy as jnp
from jax import lax

D = 1152
FF = 6912
HEADS = 4
KV_HEADS = 1
HD = 256
WINDOW = 512
TOK_DEV = 1024
PROWS = 23296
TOKENS = 32768


def draw_seg_ids(key, part):
    device_count = TOKENS // TOK_DEV
    id_most = TOK_DEV // 16 - 1
    key_live, key_cut = jax.random.split(key)
    live_slots = jax.random.randint(key_live, (device_count,), TOK_DEV // 4, TOK_DEV + 1)
    live_slots = live_slots.at[0].set(TOK_DEV).at[1].set(TOK_DEV // 2).at[2].set(TOK_DEV)
    slot_index = jnp.arange(TOK_DEV, dtype=jnp.int32)[None, :]
    cut_draw = jax.random.randint(key_cut, (device_count, TOK_DEV), 0, TOK_DEV)
    new_run = jnp.where((cut_draw < 4) | (slot_index == 0), 1, 0)
    new_run = new_run.at[0].set(jnp.where(slot_index[0] == 0, 1, 0))
    new_run = new_run.at[2].set(jnp.where(slot_index[0] % 16 == 0, 1, 0))
    run_ids = jnp.minimum(jnp.cumsum(new_run, axis=1) - 1, id_most)
    run_ids = jnp.where(slot_index < live_slots[:, None], run_ids, -1)
    return run_ids.reshape(-1).astype(jnp.int32)


def draw_params(key, part):
    key_base = jax.random.fold_in(key, 11)
    key_head = jax.random.fold_in(key, 23)
    base = jnp.clip(jax.random.normal(key_base, (PROWS, D), jnp.float32), -6.0, 6.0)
    head_factor = jnp.exp(jax.random.uniform(key_head, (HEADS,), jnp.float32, -0.4054651, 0.6931472))
    row_index = jnp.arange(PROWS, dtype=jnp.int32)
    query_rows = row_index < HEADS * HD
    key_rows = (row_index >= HEADS * HD) & (row_index < HEADS * HD + KV_HEADS * HD)
    head_of_row = jnp.minimum(row_index // HD, HEADS - 1)
    head_match = (head_of_row[:, None] == jnp.arange(HEADS, dtype=jnp.int32)[None, :]).astype(jnp.float32)
    query_factor = jnp.sum(head_match * head_factor[None, :], axis=1)
    row_factor = jnp.where(query_rows, query_factor, jnp.where(key_rows, 1.5, 1.0))
    return (base * row_factor[:, None] * D ** (-0.5)).astype(jnp.float32)


def raised(values, stream_key, source, target, parts, factor):
    owner, partner = [(jnp.arange(values.shape[position]) // (values.shape[position] // parts)).reshape([-1 if axis == position else 1 for axis in range(values.ndim)]) for position in (source, target)]
    chosen = jax.random.permutation(stream_key, parts)[partner]
    strong = (owner == chosen) | (owner == (partner + parts // 2) % parts)
    return jnp.where(strong, factor * values, values)


def shard_levels(own_key, shape, cuts, smallest, largest):
    def one(dim, shards_of):
        steps = jax.random.uniform(jax.random.fold_in(jax.random.fold_in(own_key, 6), dim), (shards_of,), jnp.float32, smallest / len(cuts), largest / len(cuts))
        return jnp.repeat(jnp.exp(steps), shape[dim] // shards_of).reshape((-1,) + (1,) * (len(shape) - dim - 1))

    loudness = one(*cuts[0])
    for cut in cuts[1:]:
        loudness = loudness * one(*cut)
    return loudness


def noise(own_key, shape, width, most, pieces=(), kind=jnp.bfloat16):
    level = shard_levels(own_key, shape, pieces, -0.22, 0.18) if pieces else 1.0
    values = jax.random.normal(own_key, shape, jnp.float32) * width * level
    return jnp.minimum(jnp.maximum(values, -most), most).astype(kind)


def heavy_noise(key, shape, deviation, most, pieces, heavy, kind=jnp.bfloat16):
    values = deviation * jax.random.normal(key, shape, jnp.float32)
    if pieces:
        values = values * shard_levels(key, shape, pieces, -0.22, 0.18)
    return jnp.clip(raised(values, jax.random.fold_in(key, 3), *heavy), -most, most).astype(kind)


def setup_inputs(seed: int = 0) -> dict:
    key_of = jax.random.split(jax.random.key(seed), 10)
    return {
        "tokens": noise(key_of[0], (TOKENS, D), 1.0, 6.0, ((0, 32),)),
        "seg_ids": draw_seg_ids(jax.random.fold_in(key_of[9], 71), 0),
        "cotangent": heavy_noise(key_of[2], (TOKENS, D), 1.0, 6.0, ((0, 32),), (0, 1, 32, 2.75)),
        "params": draw_params(jax.random.fold_in(key_of[9], 71), 0),
        "gains": jnp.clip(jax.random.uniform(key_of[4], (4, D), jnp.float32, -0.06, 0.06) * shard_levels(key_of[4], (4, D), ((1, 4),), -0.4, 0.0), -0.06, 0.06),
        "first_moment": noise(key_of[5], (PROWS, D), (0.11 * TOKENS ** 0.5), 119.47276, ((0, 4),), jnp.float32),
        "second_moment": jnp.clip(jnp.exp(math.log(6881.28) - 1.3768156 * jax.random.uniform(key_of[6], (PROWS, D), jnp.float32) ** shard_levels(key_of[6], (PROWS, D), ((0, 4),), -0.2, 0.2)), 1736.704, 6881.28),
        "gain_first": noise(key_of[7], (4, D), (0.11 * TOKENS ** 0.5), 119.47276, ((1, 4),), jnp.float32),
        "gain_second": jnp.clip(jnp.exp(math.log(6881.28) - 1.3768156 * jax.random.uniform(key_of[8], (4, D), jnp.float32) ** shard_levels(key_of[8], (4, D), ((1, 4),), -0.2, 0.2)), 1736.704, 6881.28),
    }


@jax.custom_vjp
def low(v):
    return lax.optimization_barrier(v.astype(jnp.bfloat16)).astype(jnp.float32)

@jax.custom_vjp
def low_back(v):
    return v

def low_keep(v):
    return (low(v), None)

def low_pass(kept, grad):
    return (grad,)

def back_keep(v):
    return (v, None)

def back_low(kept, grad):
    return (low(grad),)
low.defvjp(low_keep, low_pass)
low_back.defvjp(back_keep, back_low)
norm_epsilon = 1e-06
softcap_limit = 50.0
rope_base = 10000.0
beta_first = 0.9
beta_second = 0.95
learn_rate = 0.02
adam_epsilon = 1e-08
weight_decay = 0.1
adam_step = 10.0
masked_floor = -1e+30
highest = lax.Precision.HIGHEST

def rms_scale(values, gain_row):
    return values * lax.rsqrt(lax.optimization_barrier(jnp.mean(values * values, axis=-1, keepdims=True)) + norm_epsilon) * (1.0 + gain_row)

def positions_of(segments):
    index_row = jnp.arange(segments.shape[0], dtype=jnp.int32)
    previous = jnp.concatenate([segments[:1] - 1, segments[:-1]])
    first_slot = lax.cummax(jnp.where(segments != previous, index_row, 0), axis=0)
    return index_row - first_slot

def rotary_tables(positions, head_width):
    half_width = head_width // 2
    frequency = rope_base ** (-2.0 * jnp.arange(half_width, dtype=jnp.float32) / head_width)
    angles = positions.astype(jnp.float32)[:, None] * frequency[None, :]
    return (jnp.cos(angles), jnp.sin(angles))

def rotate(values, cosine_table, sine_table):
    half_width = values.shape[-1] // 2
    first_half = values[..., :half_width]
    second_half = values[..., half_width:]
    cosine_part = cosine_table[:, None, :]
    sine_part = sine_table[:, None, :]
    return jnp.concatenate([first_half * cosine_part - second_half * sine_part, second_half * cosine_part + first_half * sine_part], axis=-1)

def attend_mask(segments):
    index_row = jnp.arange(segments.shape[0], dtype=jnp.int32)
    return (segments[:, None] == segments[None, :]) & (index_row[None, :] <= index_row[:, None]) & (index_row[:, None] - index_row[None, :] < WINDOW)

def geglu(gate_value, up_value):
    return jax.nn.gelu(gate_value, approximate=True) * up_value

def block_forward(tokens_block, segments, weight_parts, gains_used):
    w_qkv, w_out, w_gate_up, w_down = weight_parts
    row_count = tokens_block.shape[0]
    query_width = HEADS * HD
    kv_width = KV_HEADS * HD
    per_group = HEADS // KV_HEADS
    cosine_table, sine_table = rotary_tables(positions_of(segments), HD)
    normed = low(rms_scale(tokens_block, gains_used[0]))
    projected = jnp.dot(normed, w_qkv.T, precision=highest)
    query_raw = low_back(projected[:, :query_width]).reshape(row_count, HEADS, HD)
    key_raw = low_back(projected[:, query_width:query_width + kv_width]).reshape(row_count, KV_HEADS, HD)
    value_heads = low(low_back(projected[:, query_width + kv_width:])).reshape(row_count, KV_HEADS, HD)
    queries = low(rotate(query_raw, cosine_table, sine_table) * HD ** (-0.5)).reshape(row_count, KV_HEADS, per_group, HD)
    key_heads = low(rotate(key_raw, cosine_table, sine_table))
    scores = low_back(jnp.einsum('qgnd,kgd->gnqk', queries, key_heads, precision=highest))
    capped = softcap_limit * jnp.tanh(scores / softcap_limit)
    allowed = attend_mask(segments)
    row_top = lax.optimization_barrier(jnp.max(jnp.where(allowed, capped, masked_floor), axis=-1, keepdims=True))
    weights_exp = jnp.where(allowed, jnp.exp(jnp.where(allowed, capped - row_top, 0.0)), 0.0)
    probability = low(weights_exp / lax.optimization_barrier(jnp.sum(weights_exp, axis=-1, keepdims=True)))
    mixed_heads = jnp.einsum('gnqk,kgd->qgnd', probability, value_heads, precision=highest)
    mixed_heads = low(low_back(mixed_heads.reshape(row_count, query_width)))
    attended = low_back(jnp.dot(mixed_heads, w_out, precision=highest))
    first_sum = tokens_block + rms_scale(attended, gains_used[1])
    ffn_input = low(rms_scale(first_sum, gains_used[2]))
    gate_up = jnp.dot(ffn_input, w_gate_up.T, precision=highest)
    hidden = low(geglu(low_back(gate_up[:, :FF]), low_back(gate_up[:, FF:])))
    branch = low_back(jnp.dot(hidden, w_down, precision=highest))
    return first_sum + rms_scale(branch, gains_used[3])

def adam_update(param_old, grad_sum, first_old, second_old, decay_rate):
    first_new = beta_first * first_old + (1.0 - beta_first) * grad_sum
    second_new = beta_second * second_old + (1.0 - beta_second) * grad_sum * grad_sum
    corrected = first_new / (1.0 - beta_first ** adam_step) / (jnp.sqrt(second_new / (1.0 - beta_second ** adam_step)) + adam_epsilon)
    return (param_old - learn_rate * (corrected + decay_rate * param_old), first_new, second_new)

def reference(tokens, seg_ids, cotangent, params, gains, first_moment, second_moment, gain_first, gain_second):
    inputs = tokens.astype(jnp.float32)
    qkv_rows = HEADS * HD + 2 * KV_HEADS * HD
    out_end = qkv_rows + HEADS * HD
    gate_end = out_end + 2 * FF

    def forward(all_tokens, all_params, all_gains):
        rows_used = low(all_params)
        gains_used = low(all_gains)
        weight_parts = (rows_used[:qkv_rows], rows_used[qkv_rows:out_end], rows_used[out_end:gate_end], rows_used[gate_end:])
        token_blocks = all_tokens.reshape(-1, TOK_DEV, D)
        segment_blocks = seg_ids.reshape(-1, TOK_DEV)

        def one_block(block_pair):
            return block_forward(block_pair[0], block_pair[1], weight_parts, gains_used)
        outputs = lax.map(jax.checkpoint(one_block), (token_blocks, segment_blocks))
        return outputs.reshape(-1, D)
    result, pullback = jax.vjp(forward, inputs, params, gains)
    input_grad, row_grad, gain_grad = pullback(cotangent.astype(jnp.float32))
    new_params, new_first, new_second = adam_update(params, row_grad, first_moment, second_moment, weight_decay)
    new_gains, new_gain_first, new_gain_second = adam_update(gains, gain_grad, gain_first, gain_second, 0.0)
    return (result.astype(jnp.bfloat16), input_grad.astype(jnp.bfloat16), row_grad, gain_grad, new_params, new_gains, new_first, new_second, new_gain_first, new_gain_second)
```

```python
import jax
import jax.numpy as jnp
from jax import lax
from jax.experimental import pallas as pl
from jax.experimental.pallas import tpu as pltpu
from jax.sharding import PartitionSpec as P

D = 1152
FF = 6912
HEADS = 4
KV_HEADS = 1
HD = 256
WINDOW = 512


norm_epsilon = 1e-06
softcap_limit = 50.0
rope_base = 10000.0
beta_first = 0.9
beta_second = 0.95
learn_rate = 0.02
adam_epsilon = 1e-08
weight_decay = 0.1
adam_step = 10.0
masked_floor = -1e30


def rms_scale(values, gain_row):
    return (
        values
        * lax.rsqrt(jnp.mean(values * values, axis=-1, keepdims=True) + norm_epsilon)
        * (1.0 + gain_row)
    )


def positions_of(segments):
    index_row = jnp.arange(segments.shape[0], dtype=jnp.int32)
    previous = jnp.concatenate([segments[:1] - 1, segments[:-1]])
    first_slot = lax.cummax(jnp.where(segments != previous, index_row, 0), axis=0)
    return index_row - first_slot


def rotary_tables(positions, head_width):
    half_width = head_width // 2
    frequency = rope_base ** (-2.0 * jnp.arange(half_width, dtype=jnp.float32) / head_width)
    angles = positions.astype(jnp.float32)[:, None] * frequency[None, :]
    return (jnp.cos(angles), jnp.sin(angles))


def rotate(values, cosine_table, sine_table):
    half_width = values.shape[-1] // 2
    first_half = values[..., :half_width]
    second_half = values[..., half_width:]
    cosine_part = cosine_table[:, None, :]
    sine_part = sine_table[:, None, :]
    return jnp.concatenate(
        [
            first_half * cosine_part - second_half * sine_part,
            second_half * cosine_part + first_half * sine_part,
        ],
        axis=-1,
    )


def geglu(gate_value, up_value):
    return jax.nn.gelu(gate_value, approximate=True) * up_value


def contract_rows(left_side, right_side):
    return lax.dot_general(
        left_side, right_side, (((0,), (0,)), ((), ())), preferred_element_type=jnp.float32
    )


def times_transposed(left_side, right_side):
    return lax.dot_general(
        left_side, right_side, (((1,), (1,)), ((), ())), preferred_element_type=jnp.float32
    )


def block_mask(query_segments, key_segments, first_row):
    query_index = first_row + jnp.arange(query_segments.shape[0], dtype=jnp.int32)
    key_index = jnp.arange(key_segments.shape[0], dtype=jnp.int32)
    return (
        (query_segments[:, None] == key_segments[None, :])
        & (key_index[None, :] <= query_index[:, None])
        & (query_index[:, None] - key_index[None, :] < WINDOW)
    )


def adam_update(param_old, grad_sum, first_old, second_old, decay_rate):
    first_new = beta_first * first_old + (1.0 - beta_first) * grad_sum
    second_new = beta_second * second_old + (1.0 - beta_second) * grad_sum * grad_sum
    corrected = (
        first_new
        / (1.0 - beta_first**adam_step)
        / (jnp.sqrt(second_new / (1.0 - beta_second**adam_step)) + adam_epsilon)
    )
    return (param_old - learn_rate * (corrected + decay_rate * param_old), first_new, second_new)


def power_of_two(count):
    return count & (count - 1) == 0


def butterfly_sum(values, axis_name):
    count = lax.axis_size(axis_name)
    if not power_of_two(count):
        return lax.psum(values, axis_name)
    step = 1
    while step < count:
        values = values + lax.ppermute(values, axis_name, [(i, i ^ step) for i in range(count)])
        step *= 2
    return values


def gather_columns(values, axis_name):
    count = lax.axis_size(axis_name)
    index = lax.axis_index(axis_name)
    width = values.shape[1]
    whole = jnp.zeros((values.shape[0], width * count), values.dtype)
    whole = lax.dynamic_update_slice_in_dim(whole, values, index * width, axis=1)
    for shift in range(1, count):
        moved = lax.ppermute(values, axis_name, [(i, (i + shift) % count) for i in range(count)])
        source = lax.rem(index + count - shift, count)
        whole = lax.dynamic_update_slice_in_dim(whole, moved, source * width, axis=1)
    return whole


def spread_first(rows):
    place = lax.axis_index("shard")
    rows = jnp.where(place == 0, rows, lax.ppermute(rows, "shard", [(0, 2)]))
    rows = jnp.where(
        lax.rem(place, 2) == 1, lax.ppermute(rows, "shard", [(0, 1), (2, 3)]), rows
    )
    index = lax.axis_index("wide")
    blocks = {0: rows}
    for bit in (4, 2, 1):
        upper = (index & bit) != 0
        grown = {}
        for key, block in blocks.items():
            other = lax.ppermute(block, "wide", [(i, i ^ bit) for i in range(8)])
            grown[key] = jnp.where(upper, other, block)
            grown[key | bit] = jnp.where(upper, block, other)
        blocks = grown
    return jnp.concatenate([blocks[key] for key in range(8)], axis=0)


owner_tree = {
    0: ([(3, 2), (1, 0)], [(2, 0)]),
    1: ([(0, 1), (3, 2)], [(2, 1)]),
    2: ([(3, 2), (0, 1)], [(1, 2)]),
    3: ([(0, 1), (2, 3)], [(1, 3)]),
}


def add_low(left, right):
    return (left.astype(jnp.float32) + right.astype(jnp.float32)).astype(left.dtype)


def tied(anchor, values):
    return lax.optimization_barrier((anchor, values))


def choose_owner(pieces):
    place = lax.axis_index("shard")
    own = pieces[0]
    for owner in range(1, len(pieces)):
        own = jnp.where(place == owner, pieces[owner], own)
    return own


def row_block(count):
    return max(size for size in range(8, 329, 8) if count % size == 0)


def adam_rows(first, grad_low, state, carried):
    count = grad_low.shape[0]
    block = row_block(count)
    spec = pl.BlockSpec((pl.Element(block), pl.Element(D)), lambda i: (pl.multiple_of(first + i * block, 8), 0))

    def body(grad_ref, param_ref, first_ref, second_ref, *rest):
        out_refs = rest[-4:]
        grad = grad_ref[...].astype(jnp.float32)
        param_new, first_new, second_new = adam_update(
            param_ref[...], grad, first_ref[...], second_ref[...], weight_decay
        )
        for ref, value in zip(out_refs, (grad, param_new, first_new, second_new)):
            ref[...] = value

    shape = jax.ShapeDtypeStruct(state[0].shape, jnp.float32)
    return pl.pallas_call(
        body,
        grid=(count // block,),
        in_specs=[pl.BlockSpec((block, D), lambda i: (i, 0))]
        + [spec] * 3
        + [pl.BlockSpec(memory_space=pl.ANY)] * len(carried),
        out_specs=[spec] * 4,
        out_shape=[shape] * 4,
        input_output_aliases={4 + k: k for k in range(len(carried))},
        cost_estimate=pl.CostEstimate(
            flops=20 * count * D, transcendentals=count * D, bytes_accessed=30 * count * D
        ),
        compiler_params=pltpu.CompilerParams(vmem_limit_bytes=48 * 2**20),
        name="adam_rows",
    )(grad_low, *state, *carried)


def per_device(
    tokens, seg_ids, cotangent, params, gains, first_moment, second_moment, gain_first, gain_second
):
    wide_count = lax.axis_size("wide")
    shard_count = lax.axis_size("shard")
    owner_rows = params.shape[0]
    total_rows = owner_rows * shard_count
    early_rows = (HEADS + 2 * KV_HEADS) * HD + HEADS * HD
    wide_index = lax.axis_index("wide")

    def own_slice(first, count):
        part = count // wide_count
        return lax.dynamic_slice_in_dim(
            params, first + wide_index * part, part, axis=0
        ).astype(jnp.bfloat16)

    rows_used = lax.all_gather(own_slice(0, owner_rows), ("shard", "wide"), axis=0, tiled=True)
    if wide_count == 8 and shard_count == 4:
        early_used = spread_first(own_slice(0, early_rows))
    else:
        early_used = rows_used[:early_rows]
    gains_used = gather_columns(gains.astype(jnp.bfloat16), "shard")
    gains_float = gains_used.astype(jnp.float32)
    query_width = HEADS * HD
    kv_width = KV_HEADS * HD
    per_group = HEADS // KV_HEADS
    qkv_rows = query_width + 2 * kv_width
    out_end = qkv_rows + query_width
    gate_end = out_end + 2 * FF
    w_qkv = early_used[:qkv_rows]
    w_out = early_used[qkv_rows:out_end]
    w_gate_up = rows_used[out_end:gate_end]
    w_down = rows_used[gate_end:]
    row_count = tokens.shape[0]
    block_rows = min(512, row_count)
    block_count = row_count // block_rows
    query_scale = HD ** (-0.5)
    inputs = tokens.astype(jnp.float32)
    cosine_table, sine_table = rotary_tables(positions_of(seg_ids), HD)
    normed, pull_first = jax.vjp(rms_scale, inputs, gains_float[0])
    normed_low = normed.astype(jnp.bfloat16)
    projected = times_transposed(normed_low, w_qkv)
    query_raw = projected[:, :query_width].reshape(row_count, HEADS, HD)
    key_raw = projected[:, query_width : query_width + kv_width].reshape(row_count, KV_HEADS, HD)
    value_heads = (
        projected[:, query_width + kv_width :].astype(jnp.bfloat16).reshape(row_count, KV_HEADS, HD)
    )
    queries = (rotate(query_raw, cosine_table, sine_table) * query_scale).astype(jnp.bfloat16)
    key_heads = rotate(key_raw, cosine_table, sine_table).astype(jnp.bfloat16)
    query_blocks = queries.reshape(block_count, block_rows, KV_HEADS, per_group, HD)
    segment_blocks = seg_ids.reshape(block_count, block_rows)
    block_starts = jnp.arange(block_count, dtype=jnp.int32) * block_rows

    def forward_block(inputs_block):
        query_block, segment_block, first_row = inputs_block
        scores = jnp.einsum(
            "qgnd,kgd->gnqk", query_block, key_heads, preferred_element_type=jnp.float32
        )
        capped = softcap_limit * jnp.tanh(scores / softcap_limit)
        allowed = block_mask(segment_block, seg_ids, first_row)
        row_top = jnp.max(jnp.where(allowed, capped, masked_floor), axis=-1, keepdims=True)
        weights_exp = jnp.where(allowed, jnp.exp(jnp.where(allowed, capped - row_top, 0.0)), 0.0)
        totals = jnp.sum(weights_exp, axis=-1, keepdims=True)
        probability = (weights_exp / totals).astype(jnp.bfloat16)
        mixed_block = jnp.einsum(
            "gnqk,kgd->qgnd", probability, value_heads, preferred_element_type=jnp.float32
        )
        return (mixed_block, row_top + jnp.log(totals))

    mixed_heads, log_totals = lax.map(forward_block, (query_blocks, segment_blocks, block_starts))
    mixed_low = mixed_heads.reshape(row_count, query_width).astype(jnp.bfloat16)
    attended = jnp.dot(mixed_low, w_out, preferred_element_type=jnp.float32)
    attn_normed, pull_second = jax.vjp(rms_scale, attended, gains_float[1])
    first_sum = inputs + attn_normed
    ffn_input, pull_third = jax.vjp(rms_scale, first_sum, gains_float[2])
    ffn_low = ffn_input.astype(jnp.bfloat16)
    gate_up = times_transposed(ffn_low, w_gate_up)
    hidden, pull_fourth = jax.vjp(geglu, gate_up[:, :FF], gate_up[:, FF:])
    hidden_low = hidden.astype(jnp.bfloat16)
    branch = jnp.dot(hidden_low, w_down, preferred_element_type=jnp.float32)
    ffn_normed, pull_fifth = jax.vjp(rms_scale, branch, gains_float[3])
    result = first_sum + ffn_normed
    upstream = cotangent.astype(jnp.float32)
    branch_grad, gain_four = pull_fifth(upstream)
    branch_low = branch_grad.astype(jnp.bfloat16)
    tree = wide_count == 8 and shard_count == 4
    factors = {"down": (gate_end, total_rows, hidden_low, branch_low)}
    reduced, steps = {}, {}

    def bounds(owner, part):
        edges = (0, early_rows, owner_rows)
        return owner * owner_rows + edges[part], owner * owner_rows + edges[part + 1]

    def plane_terms(first, last):
        parts = [
            contract_rows(
                left[:, max(first, start) - start : min(last, end) - start], right
            ).astype(jnp.bfloat16)
            for start, end, left, right in sorted(factors.values(), key=lambda f: f[0])
            if max(first, start) < min(last, end)
        ]
        return parts[0] if len(parts) == 1 else jnp.concatenate(parts, axis=0)

    def plane_sum(first, last):
        return lax.psum_scatter(
            plane_terms(first, last), "wide", scatter_dimension=0, tiled=True
        )

    def start_ready(anchor, lowest):
        keys = [
            (owner, part)
            for part in (1, 0)
            for owner in range(shard_count)
            if (owner, part) not in reduced and bounds(owner, part)[0] >= lowest
        ]
        terms = [plane_terms(*bounds(*key)) for key in keys]
        for key, term in zip(keys, terms):
            reduced[key] = lax.psum_scatter(term, "wide", scatter_dimension=0, tiled=True)
            steps[key] = [reduced[key]]
        return tied(anchor, terms)[0]

    def advance(key):
        owner, _ = key
        pairs = owner_tree[owner][len(steps[key]) - 1]
        held = steps[key][-1]
        steps[key].append(add_low(held, lax.ppermute(held, "shard", pairs)))

    def tick(anchor, *keys):
        if not tree:
            return anchor
        anchor, values = tied(anchor, [steps[key][-1] for key in keys])
        for key, value in zip(keys, values):
            steps[key][-1] = value
            advance(key)
        return anchor

    branch_low = start_ready(branch_low, gate_end)
    hidden_grad = times_transposed(branch_low, w_down)
    gate_grad, up_grad = pull_fourth(hidden_grad)
    gate_up_low = jnp.concatenate([gate_grad, up_grad], axis=1).astype(jnp.bfloat16)
    factors["gate_up"] = (out_end, gate_end, gate_up_low, ffn_low)
    gate_up_low = start_ready(gate_up_low, out_end)
    gate_up_low = tick(gate_up_low, (3, 1), (3, 0))
    ffn_input_grad = jnp.dot(gate_up_low, w_gate_up, preferred_element_type=jnp.float32)
    ffn_input_grad = tick(ffn_input_grad, (3, 1), (3, 0), (0, 1))
    sum_grad_part, gain_three = pull_third(ffn_input_grad)
    sum_grad = upstream + sum_grad_part
    attended_grad, gain_two = pull_second(sum_grad)
    attended_low = attended_grad.astype(jnp.bfloat16)
    factors["out"] = (qkv_rows, out_end, mixed_low, attended_low)
    mixed_grad = (
        times_transposed(attended_low, w_out)
        .astype(jnp.bfloat16)
        .reshape(block_count, block_rows, KV_HEADS, per_group, HD)
    )

    mixed_grad = tick(mixed_grad, (0, 1), (1, 1))

    def backward_block(running, inputs_block):
        key_acc, value_acc = running
        query_block, grad_block, segment_block, first_row, log_block = inputs_block
        scores = jnp.einsum(
            "qgnd,kgd->gnqk", query_block, key_heads, preferred_element_type=jnp.float32
        )
        capped = softcap_limit * jnp.tanh(scores / softcap_limit)
        allowed = block_mask(segment_block, seg_ids, first_row)
        probability = jnp.where(allowed, jnp.exp(jnp.where(allowed, capped - log_block, 0.0)), 0.0)
        probability_low = probability.astype(jnp.bfloat16)
        value_acc = value_acc + jnp.einsum(
            "gnqk,qgnd->kgd", probability_low, grad_block, preferred_element_type=jnp.float32
        )
        prob_grad = jnp.einsum(
            "qgnd,kgd->gnqk", grad_block, value_heads, preferred_element_type=jnp.float32
        )
        centred = jnp.sum(probability * prob_grad, axis=-1, keepdims=True)
        score_grad = (
            probability * (prob_grad - centred) * (1.0 - (capped / softcap_limit) ** 2)
        ).astype(jnp.bfloat16)
        query_grad_block = jnp.einsum(
            "gnqk,kgd->qgnd", score_grad, key_heads, preferred_element_type=jnp.float32
        )
        key_acc = key_acc + jnp.einsum(
            "gnqk,qgnd->kgd", score_grad, query_block, preferred_element_type=jnp.float32
        )
        return ((key_acc, value_acc), query_grad_block)

    zero_heads = jnp.zeros((row_count, KV_HEADS, HD), jnp.float32)
    (key_grad, value_grad), query_grad = lax.scan(
        backward_block,
        (zero_heads, zero_heads),
        (query_blocks, mixed_grad, segment_blocks, block_starts, log_totals),
    )
    query_grad = tick(query_grad, (1, 1), (2, 1))
    query_raw_grad = rotate(
        query_grad.reshape(row_count, HEADS, HD) * query_scale, cosine_table, -sine_table
    )
    key_raw_grad = rotate(key_grad, cosine_table, -sine_table)
    qkv_low = jnp.concatenate(
        [
            query_raw_grad.reshape(row_count, query_width),
            key_raw_grad.reshape(row_count, kv_width),
            value_grad.reshape(row_count, kv_width),
        ],
        axis=1,
    ).astype(jnp.bfloat16)
    factors["qkv"] = (0, qkv_rows, qkv_low, normed_low)
    normed_grad = jnp.dot(qkv_low, w_qkv, preferred_element_type=jnp.float32)
    input_part, gain_one = pull_first(normed_grad)
    input_grad = sum_grad + input_part
    reduced[0, 0] = plane_sum(0, early_rows)
    steps[0, 0] = [reduced[0, 0]]
    if tree:
        for key in sorted(reduced, key=lambda k: k[1], reverse=True):
            while len(steps[key]) < 3:
                advance(key)
        late_piece = choose_owner([steps[owner, 1][-1] for owner in range(shard_count)])
        early_piece = choose_owner([steps[owner, 0][-1] for owner in range(shard_count)])
    else:
        late_piece, early_piece = [
            lax.psum_scatter(
                jnp.concatenate([reduced[owner, part] for owner in range(shard_count)], axis=0),
                "shard",
                scatter_dimension=0,
                tiled=True,
            )
            for part in (1, 0)
        ]
    late_low = lax.all_gather(late_piece, "wide", axis=0, tiled=True)
    early_low = lax.all_gather(early_piece, "wide", axis=0, tiled=True)
    state = (params, first_moment, second_moment)
    carried = adam_rows(early_rows, late_low, state, ())
    row_grad, new_params, new_first, new_second = adam_rows(0, early_low, state, carried)
    gain_terms = jnp.stack([gain_one, gain_two, gain_three, gain_four])
    gain_total = butterfly_sum(butterfly_sum(gain_terms, "wide"), "shard")
    gain_grad = lax.dynamic_slice_in_dim(
        gain_total, lax.axis_index("shard") * gains.shape[1], gains.shape[1], axis=1
    )
    new_gains, new_gain_first, new_gain_second = adam_update(
        gains, gain_grad, gain_first, gain_second, 0.0
    )
    return (
        result.astype(jnp.bfloat16),
        input_grad.astype(jnp.bfloat16),
        row_grad,
        gain_grad,
        new_params,
        new_gains,
        new_first,
        new_second,
        new_gain_first,
        new_gain_second,
    )


def solution(mesh):
    return jax.shard_map(
        per_device,
        mesh=mesh,
        in_specs=(
            P(("wide", "shard"), None),
            P(("wide", "shard")),
            P(("wide", "shard"), None),
            P("shard", None),
            P(None, "shard"),
            P("shard", None),
            P("shard", None),
            P(None, "shard"),
            P(None, "shard"),
        ),
        out_specs=(
            P(("wide", "shard"), None),
            P(("wide", "shard"), None),
            P("shard", None),
            P(None, "shard"),
            P("shard", None),
            P(None, "shard"),
            P("shard", None),
            P("shard", None),
            P(None, "shard"),
            P(None, "shard"),
        ),
        check_vma=False,
    )
```

```python
import jax
import jax.numpy as jnp
from jax import lax
from jax.experimental import pallas as pl
from jax.experimental.pallas import tpu as pltpu
from jax.sharding import PartitionSpec as P

D = 1152
FF = 6912
HEADS = 4
KV_HEADS = 1
HD = 256
WINDOW = 512


norm_epsilon = 1e-06
softcap_limit = 50.0
rope_base = 10000.0
beta_first = 0.9
beta_second = 0.95
learn_rate = 0.02
adam_epsilon = 1e-08
weight_decay = 0.1
adam_step = 10.0
masked_floor = -1e30


def rms_scale(values, gain_row):
    return (
        values
        * lax.rsqrt(jnp.mean(values * values, axis=-1, keepdims=True) + norm_epsilon)
        * (1.0 + gain_row)
    )


def positions_of(segments):
    index_row = jnp.arange(segments.shape[0], dtype=jnp.int32)
    previous = jnp.concatenate([segments[:1] - 1, segments[:-1]])
    first_slot = lax.cummax(jnp.where(segments != previous, index_row, 0), axis=0)
    return index_row - first_slot


def rotary_tables(positions, head_width):
    half_width = head_width // 2
    frequency = rope_base ** (-2.0 * jnp.arange(half_width, dtype=jnp.float32) / head_width)
    angles = positions.astype(jnp.float32)[:, None] * frequency[None, :]
    return (jnp.cos(angles), jnp.sin(angles))


def rotate(values, cosine_table, sine_table):
    half_width = values.shape[-1] // 2
    first_half = values[..., :half_width]
    second_half = values[..., half_width:]
    cosine_part = cosine_table[:, None, :]
    sine_part = sine_table[:, None, :]
    return jnp.concatenate(
        [
            first_half * cosine_part - second_half * sine_part,
            second_half * cosine_part + first_half * sine_part,
        ],
        axis=-1,
    )


def geglu(gate_value, up_value):
    return jax.nn.gelu(gate_value, approximate=True) * up_value


def contract_rows(left_side, right_side):
    return lax.dot_general(
        left_side, right_side, (((0,), (0,)), ((), ())), preferred_element_type=jnp.float32
    )


def times_transposed(left_side, right_side):
    return lax.dot_general(
        left_side, right_side, (((1,), (1,)), ((), ())), preferred_element_type=jnp.float32
    )


def block_mask(query_segments, key_segments, first_row):
    query_index = first_row + jnp.arange(query_segments.shape[0], dtype=jnp.int32)
    key_index = jnp.arange(key_segments.shape[0], dtype=jnp.int32)
    return (
        (query_segments[:, None] == key_segments[None, :])
        & (key_index[None, :] <= query_index[:, None])
        & (query_index[:, None] - key_index[None, :] < WINDOW)
    )


def adam_update(param_old, grad_sum, first_old, second_old, decay_rate):
    first_new = beta_first * first_old + (1.0 - beta_first) * grad_sum
    second_new = beta_second * second_old + (1.0 - beta_second) * grad_sum * grad_sum
    corrected = (
        first_new
        / (1.0 - beta_first**adam_step)
        / (jnp.sqrt(second_new / (1.0 - beta_second**adam_step)) + adam_epsilon)
    )
    return (param_old - learn_rate * (corrected + decay_rate * param_old), first_new, second_new)


def power_of_two(count):
    return count & (count - 1) == 0


def butterfly_sum(values, axis_name):
    count = lax.axis_size(axis_name)
    if not power_of_two(count):
        return lax.psum(values, axis_name)
    step = 1
    while step < count:
        values = values + lax.ppermute(values, axis_name, [(i, i ^ step) for i in range(count)])
        step *= 2
    return values


def gather_columns(values, axis_name):
    count = lax.axis_size(axis_name)
    index = lax.axis_index(axis_name)
    width = values.shape[1]
    whole = jnp.zeros((values.shape[0], width * count), values.dtype)
    whole = lax.dynamic_update_slice_in_dim(whole, values, index * width, axis=1)
    for shift in range(1, count):
        moved = lax.ppermute(values, axis_name, [(i, (i + shift) % count) for i in range(count)])
        source = lax.rem(index + count - shift, count)
        whole = lax.dynamic_update_slice_in_dim(whole, moved, source * width, axis=1)
    return whole


def spread_first(rows):
    place = lax.axis_index("shard")
    rows = jnp.where(place == 0, rows, lax.ppermute(rows, "shard", [(0, 2)]))
    rows = jnp.where(
        lax.rem(place, 2) == 1, lax.ppermute(rows, "shard", [(0, 1), (2, 3)]), rows
    )
    index = lax.axis_index("wide")
    blocks = {0: rows}
    for bit in (4, 2, 1):
        upper = (index & bit) != 0
        grown = {}
        for key, block in blocks.items():
            other = lax.ppermute(block, "wide", [(i, i ^ bit) for i in range(8)])
            grown[key] = jnp.where(upper, other, block)
            grown[key | bit] = jnp.where(upper, block, other)
        blocks = grown
    return jnp.concatenate([blocks[key] for key in range(8)], axis=0)


owner_tree = {
    0: ([(3, 2), (1, 0)], [(2, 0)]),
    1: ([(0, 1), (3, 2)], [(2, 1)]),
    2: ([(3, 2), (0, 1)], [(1, 2)]),
    3: ([(0, 1), (2, 3)], [(1, 3)]),
}


def add_low(left, right):
    return (left.astype(jnp.float32) + right.astype(jnp.float32)).astype(left.dtype)


def tied(anchor, values):
    return lax.optimization_barrier((anchor, values))


def choose_owner(pieces):
    place = lax.axis_index("shard")
    own = pieces[0]
    for owner in range(1, len(pieces)):
        own = jnp.where(place == owner, pieces[owner], own)
    return own


def adam_rows(place, block, grad_low, state, carried):
    count = grad_low.shape[0]

    def rows_of(i, place_ref):
        return (pl.multiple_of(place_ref[0] + i * place_ref[1], 8), 0)

    spec = pl.BlockSpec((pl.Element(block), pl.Element(D)), rows_of)

    def body(place_ref, grad_ref, param_ref, first_ref, second_ref, *rest):
        out_refs = rest[-4:]
        grad = grad_ref[...].astype(jnp.float32)
        param_new, first_new, second_new = adam_update(
            param_ref[...], grad, first_ref[...], second_ref[...], weight_decay
        )
        for ref, value in zip(out_refs, (grad, param_new, first_new, second_new)):
            ref[...] = value

    shape = jax.ShapeDtypeStruct(state[0].shape, jnp.float32)
    return pl.pallas_call(
        body,
        grid_spec=pltpu.PrefetchScalarGridSpec(
            num_scalar_prefetch=1,
            grid=(count // block,),
            in_specs=[pl.BlockSpec((block, D), lambda i, place_ref: (i, 0))]
            + [spec] * 3
            + [pl.BlockSpec(memory_space=pl.ANY)] * len(carried),
            out_specs=[spec] * 4,
        ),
        out_shape=[shape] * 4,
        input_output_aliases={5 + k: k for k in range(len(carried))},
        cost_estimate=pl.CostEstimate(
            flops=20 * count * D, transcendentals=count * D, bytes_accessed=30 * count * D
        ),
        compiler_params=pltpu.CompilerParams(vmem_limit_bytes=56 * 2**20),
        name="adam_rows",
    )(place, grad_low, *state, *carried)


def per_device(
    tokens, seg_ids, cotangent, params, gains, first_moment, second_moment, gain_first, gain_second
):
    wide_count = lax.axis_size("wide")
    shard_count = lax.axis_size("shard")
    owner_rows = params.shape[0]
    total_rows = owner_rows * shard_count
    early_rows = (HEADS + 2 * KV_HEADS) * HD + HEADS * HD
    wide_index = lax.axis_index("wide")

    def own_slice(first, count):
        part = count // wide_count
        return lax.dynamic_slice_in_dim(
            params, first + wide_index * part, part, axis=0
        ).astype(jnp.bfloat16)

    rows_used = lax.all_gather(own_slice(0, owner_rows), ("shard", "wide"), axis=0, tiled=True)
    if wide_count == 8 and shard_count == 4:
        early_used = spread_first(own_slice(0, early_rows))
    else:
        early_used = rows_used[:early_rows]
    gains_used = gather_columns(gains.astype(jnp.bfloat16), "shard")
    gains_float = gains_used.astype(jnp.float32)
    query_width = HEADS * HD
    kv_width = KV_HEADS * HD
    per_group = HEADS // KV_HEADS
    qkv_rows = query_width + 2 * kv_width
    out_end = qkv_rows + query_width
    gate_end = out_end + 2 * FF
    w_qkv = early_used[:qkv_rows]
    w_out = early_used[qkv_rows:out_end]
    w_gate_up = rows_used[out_end:gate_end]
    w_down = rows_used[gate_end:]
    row_count = tokens.shape[0]
    block_rows = min(512, row_count)
    block_count = row_count // block_rows
    query_scale = HD ** (-0.5)
    inputs = tokens.astype(jnp.float32)
    cosine_table, sine_table = rotary_tables(positions_of(seg_ids), HD)
    normed, pull_first = jax.vjp(rms_scale, inputs, gains_float[0])
    normed_low = normed.astype(jnp.bfloat16)
    projected = times_transposed(normed_low, w_qkv)
    query_raw = projected[:, :query_width].reshape(row_count, HEADS, HD)
    key_raw = projected[:, query_width : query_width + kv_width].reshape(row_count, KV_HEADS, HD)
    value_heads = (
        projected[:, query_width + kv_width :].astype(jnp.bfloat16).reshape(row_count, KV_HEADS, HD)
    )
    queries = (rotate(query_raw, cosine_table, sine_table) * query_scale).astype(jnp.bfloat16)
    key_heads = rotate(key_raw, cosine_table, sine_table).astype(jnp.bfloat16)
    query_blocks = queries.reshape(block_count, block_rows, KV_HEADS, per_group, HD)
    segment_blocks = seg_ids.reshape(block_count, block_rows)
    block_starts = jnp.arange(block_count, dtype=jnp.int32) * block_rows

    def forward_block(inputs_block):
        query_block, segment_block, first_row = inputs_block
        scores = jnp.einsum(
            "qgnd,kgd->gnqk", query_block, key_heads, preferred_element_type=jnp.float32
        )
        capped = softcap_limit * jnp.tanh(scores / softcap_limit)
        allowed = block_mask(segment_block, seg_ids, first_row)
        row_top = jnp.max(jnp.where(allowed, capped, masked_floor), axis=-1, keepdims=True)
        weights_exp = jnp.where(allowed, jnp.exp(jnp.where(allowed, capped - row_top, 0.0)), 0.0)
        totals = jnp.sum(weights_exp, axis=-1, keepdims=True)
        probability = (weights_exp / totals).astype(jnp.bfloat16)
        mixed_block = jnp.einsum(
            "gnqk,kgd->qgnd", probability, value_heads, preferred_element_type=jnp.float32
        )
        return (mixed_block, row_top + jnp.log(totals))

    mixed_heads, log_totals = lax.map(forward_block, (query_blocks, segment_blocks, block_starts))
    mixed_low = mixed_heads.reshape(row_count, query_width).astype(jnp.bfloat16)
    attended = jnp.dot(mixed_low, w_out, preferred_element_type=jnp.float32)
    attn_normed, pull_second = jax.vjp(rms_scale, attended, gains_float[1])
    first_sum = inputs + attn_normed
    ffn_input, pull_third = jax.vjp(rms_scale, first_sum, gains_float[2])
    ffn_low = ffn_input.astype(jnp.bfloat16)
    gate_up = times_transposed(ffn_low, w_gate_up)
    hidden, pull_fourth = jax.vjp(geglu, gate_up[:, :FF], gate_up[:, FF:])
    hidden_low = hidden.astype(jnp.bfloat16)
    branch = jnp.dot(hidden_low, w_down, preferred_element_type=jnp.float32)
    ffn_normed, pull_fifth = jax.vjp(rms_scale, branch, gains_float[3])
    result = first_sum + ffn_normed
    upstream = cotangent.astype(jnp.float32)
    branch_grad, gain_four = pull_fifth(upstream)
    branch_low = branch_grad.astype(jnp.bfloat16)
    tree = wide_count == 8 and shard_count == 4
    factors = {"down": (gate_end, total_rows, hidden_low, branch_low)}
    steps = {}
    late_rows = qkv_rows

    def bounds(key):
        return (max(key * owner_rows, late_rows), (key + 1) * owner_rows)

    def plane_terms(first, last):
        parts = [
            contract_rows(
                left[:, max(first, start) - start : min(last, end) - start], right
            ).astype(jnp.bfloat16)
            for start, end, left, right in sorted(factors.values(), key=lambda f: f[0])
            if max(first, start) < min(last, end)
        ]
        return parts[0] if len(parts) == 1 else jnp.concatenate(parts, axis=0)

    def start_ready(anchor, lowest):
        keys = [
            key
            for key in reversed(range(shard_count))
            if key not in steps and bounds(key)[0] >= lowest
        ]
        if not tree or not keys:
            return anchor
        terms = [plane_terms(*bounds(key)) for key in keys]
        for key, term in zip(keys, terms):
            steps[key] = [lax.psum_scatter(term, "wide", scatter_dimension=0, tiled=True)]
        return tied(anchor, terms)[0]

    def advance(key):
        pairs = owner_tree[max(key, 0)][len(steps[key]) - 1]
        held = steps[key][-1]
        steps[key].append(add_low(held, lax.ppermute(held, "shard", pairs)))

    def tick(anchor, *keys):
        if not tree:
            return anchor
        anchor, values = tied(anchor, [steps[key][-1] for key in keys])
        for key, value in zip(keys, values):
            steps[key][-1] = value
            advance(key)
        return anchor

    branch_low = start_ready(branch_low, gate_end)
    hidden_grad = times_transposed(branch_low, w_down)
    gate_grad, up_grad = pull_fourth(hidden_grad)
    gate_low, up_low = gate_grad.astype(jnp.bfloat16), up_grad.astype(jnp.bfloat16)
    factors["gate"] = (out_end, out_end + FF, gate_low, ffn_low)
    factors["up"] = (out_end + FF, gate_end, up_low, ffn_low)
    gate_low, up_low = start_ready((gate_low, up_low), out_end)
    gate_low, up_low = tick((gate_low, up_low), 3)
    ffn_input_grad = jnp.dot(
        gate_low, w_gate_up[:FF], preferred_element_type=jnp.float32
    ) + jnp.dot(up_low, w_gate_up[FF:], preferred_element_type=jnp.float32)
    ffn_input_grad = tick(ffn_input_grad, 3)
    sum_grad_part, gain_three = pull_third(ffn_input_grad)
    sum_grad = upstream + sum_grad_part
    attended_grad, gain_two = pull_second(sum_grad)
    attended_low = attended_grad.astype(jnp.bfloat16)
    factors["out"] = (qkv_rows, out_end, mixed_low, attended_low)
    mixed_grad = (
        times_transposed(attended_low, w_out)
        .astype(jnp.bfloat16)
        .reshape(block_count, block_rows, KV_HEADS, per_group, HD)
    )

    mixed_grad = start_ready(mixed_grad, late_rows)
    mixed_grad = tick(mixed_grad, 2)

    def backward_block(running, inputs_block):
        key_acc, value_acc = running
        query_block, grad_block, segment_block, first_row, log_block = inputs_block
        scores = jnp.einsum(
            "qgnd,kgd->gnqk", query_block, key_heads, preferred_element_type=jnp.float32
        )
        capped = softcap_limit * jnp.tanh(scores / softcap_limit)
        allowed = block_mask(segment_block, seg_ids, first_row)
        probability = jnp.where(allowed, jnp.exp(jnp.where(allowed, capped - log_block, 0.0)), 0.0)
        probability_low = probability.astype(jnp.bfloat16)
        value_acc = value_acc + jnp.einsum(
            "gnqk,qgnd->kgd", probability_low, grad_block, preferred_element_type=jnp.float32
        )
        prob_grad = jnp.einsum(
            "qgnd,kgd->gnqk", grad_block, value_heads, preferred_element_type=jnp.float32
        )
        centred = jnp.sum(probability * prob_grad, axis=-1, keepdims=True)
        score_grad = (
            probability * (prob_grad - centred) * (1.0 - (capped / softcap_limit) ** 2)
        ).astype(jnp.bfloat16)
        query_grad_block = jnp.einsum(
            "gnqk,kgd->qgnd", score_grad, key_heads, preferred_element_type=jnp.float32
        )
        key_acc = key_acc + jnp.einsum(
            "gnqk,qgnd->kgd", score_grad, query_block, preferred_element_type=jnp.float32
        )
        return ((key_acc, value_acc), query_grad_block)

    zero_heads = jnp.zeros((row_count, KV_HEADS, HD), jnp.float32)
    (key_grad, value_grad), query_grad = lax.scan(
        backward_block,
        (zero_heads, zero_heads),
        (query_blocks, mixed_grad, segment_blocks, block_starts, log_totals),
    )
    query_grad = tick(query_grad, 2, 1)
    query_raw_grad = rotate(
        query_grad.reshape(row_count, HEADS, HD) * query_scale, cosine_table, -sine_table
    )
    key_raw_grad = rotate(key_grad, cosine_table, -sine_table)
    qkv_low = jnp.concatenate(
        [
            query_raw_grad.reshape(row_count, query_width),
            key_raw_grad.reshape(row_count, kv_width),
            value_grad.reshape(row_count, kv_width),
        ],
        axis=1,
    ).astype(jnp.bfloat16)
    factors["qkv"] = (0, qkv_rows, qkv_low, normed_low)
    normed_grad = jnp.dot(qkv_low, w_qkv, preferred_element_type=jnp.float32)
    input_part, gain_one = pull_first(normed_grad)
    input_grad = sum_grad + input_part
    state = (params, first_moment, second_moment)
    if tree:
        steps[-1] = [
            lax.psum_scatter(plane_terms(0, late_rows), "wide", scatter_dimension=0, tiled=True)
        ]
        for key in (3, 2, 1, 0, -1):
            while len(steps[key]) < 3:
                advance(key)
        late_part = late_rows // wide_count
        early_part = owner_rows // wide_count - late_part
        whole_pieces = [steps[owner][-1] for owner in range(1, shard_count)]
        early_piece = choose_owner([steps[0][-1]] + [p[:early_part] for p in whole_pieces])
        late_piece = choose_owner([steps[-1][-1]] + [p[early_part:] for p in whole_pieces])
        first_owner = lax.axis_index("shard") == 0
        early_place = jnp.where(
            first_owner,
            jnp.array([late_rows, early_part], jnp.int32),
            jnp.array([0, early_part + late_part], jnp.int32),
        )
        late_place = jnp.where(
            first_owner,
            jnp.array([0, late_part], jnp.int32),
            jnp.array([early_part, early_part + late_part], jnp.int32),
        )
        early_low = lax.all_gather(early_piece, "wide", axis=0, tiled=True)
        late_low = lax.all_gather(late_piece, "wide", axis=0, tiled=True)
        carried = adam_rows(early_place, early_part, early_low, state, ())
        row_grad, new_params, new_first, new_second = adam_rows(
            late_place, late_part, late_low, state, carried
        )
    else:
        own = lax.psum_scatter(
            plane_terms(0, total_rows), ("shard", "wide"), scatter_dimension=0, tiled=True
        )
        own_low = lax.all_gather(own, "wide", axis=0, tiled=True)
        block = max(size for size in range(8, 329, 8) if owner_rows % size == 0)
        row_grad, new_params, new_first, new_second = adam_rows(
            jnp.array([0, block], jnp.int32), block, own_low, state, ()
        )
    gain_terms = jnp.stack([gain_one, gain_two, gain_three, gain_four])
    gain_total = butterfly_sum(butterfly_sum(gain_terms, "wide"), "shard")
    gain_grad = lax.dynamic_slice_in_dim(
        gain_total, lax.axis_index("shard") * gains.shape[1], gains.shape[1], axis=1
    )
    new_gains, new_gain_first, new_gain_second = adam_update(
        gains, gain_grad, gain_first, gain_second, 0.0
    )
    return (
        result.astype(jnp.bfloat16),
        input_grad.astype(jnp.bfloat16),
        row_grad,
        gain_grad,
        new_params,
        new_gains,
        new_first,
        new_second,
        new_gain_first,
        new_gain_second,
    )


def solution(mesh):
    return jax.shard_map(
        per_device,
        mesh=mesh,
        in_specs=(
            P(("wide", "shard"), None),
            P(("wide", "shard")),
            P(("wide", "shard"), None),
            P("shard", None),
            P(None, "shard"),
            P("shard", None),
            P("shard", None),
            P(None, "shard"),
            P(None, "shard"),
        ),
        out_specs=(
            P(("wide", "shard"), None),
            P(("wide", "shard"), None),
            P("shard", None),
            P(None, "shard"),
            P("shard", None),
            P(None, "shard"),
            P("shard", None),
            P("shard", None),
            P(None, "shard"),
            P(None, "shard"),
        ),
        check_vma=False,
    )
```

```python
import jax
import jax.numpy as jnp
from jax import lax
from jax.experimental import pallas as pl
from jax.experimental.pallas import tpu as pltpu
from jax.sharding import Mesh
from jax.sharding import PartitionSpec as P

D = 1152
FF = 6912
HEADS = 4
KV_HEADS = 1
HD = 256
WINDOW = 512


norm_epsilon = 1e-06
softcap_limit = 50.0
rope_base = 10000.0
beta_first = 0.9
beta_second = 0.95
learn_rate = 0.02
adam_epsilon = 1e-08
weight_decay = 0.1
adam_step = 10.0
masked_floor = -1e30


def rms_scale(values, gain_row):
    return (
        values
        * lax.rsqrt(jnp.mean(values * values, axis=-1, keepdims=True) + norm_epsilon)
        * (1.0 + gain_row)
    )


def positions_of(segments):
    index_row = jnp.arange(segments.shape[0], dtype=jnp.int32)
    previous = jnp.concatenate([segments[:1] - 1, segments[:-1]])
    first_slot = lax.cummax(jnp.where(segments != previous, index_row, 0), axis=0)
    return index_row - first_slot


def rotary_tables(positions, head_width):
    half_width = head_width // 2
    frequency = rope_base ** (-2.0 * jnp.arange(half_width, dtype=jnp.float32) / head_width)
    angles = positions.astype(jnp.float32)[:, None] * frequency[None, :]
    return (jnp.cos(angles), jnp.sin(angles))


def rotate(values, cosine_table, sine_table):
    half_width = values.shape[-1] // 2
    first_half = values[..., :half_width]
    second_half = values[..., half_width:]
    cosine_part = cosine_table[:, None, :]
    sine_part = sine_table[:, None, :]
    return jnp.concatenate(
        [
            first_half * cosine_part - second_half * sine_part,
            second_half * cosine_part + first_half * sine_part,
        ],
        axis=-1,
    )


def geglu(gate_value, up_value):
    return jax.nn.gelu(gate_value, approximate=True) * up_value


def contract_rows(left_side, right_side):
    return lax.dot_general(
        left_side, right_side, (((0,), (0,)), ((), ())), preferred_element_type=jnp.float32
    )


def times_transposed(left_side, right_side):
    return lax.dot_general(
        left_side, right_side, (((1,), (1,)), ((), ())), preferred_element_type=jnp.float32
    )


def block_mask(query_segments, key_segments, first_row):
    query_index = first_row + jnp.arange(query_segments.shape[0], dtype=jnp.int32)
    key_index = jnp.arange(key_segments.shape[0], dtype=jnp.int32)
    return (
        (query_segments[:, None] == key_segments[None, :])
        & (key_index[None, :] <= query_index[:, None])
        & (query_index[:, None] - key_index[None, :] < WINDOW)
    )


def adam_update(param_old, grad_sum, first_old, second_old, decay_rate):
    first_new = beta_first * first_old + (1.0 - beta_first) * grad_sum
    second_new = beta_second * second_old + (1.0 - beta_second) * grad_sum * grad_sum
    corrected = (
        first_new
        / (1.0 - beta_first**adam_step)
        / (jnp.sqrt(second_new / (1.0 - beta_second**adam_step)) + adam_epsilon)
    )
    return (param_old - learn_rate * (corrected + decay_rate * param_old), first_new, second_new)


def power_of_two(count):
    return count & (count - 1) == 0


WIDE = ("chip", "core")


def wide_size():
    return lax.axis_size("chip") * lax.axis_size("core")


def butterfly_sum(values, axis_name, count):
    if not power_of_two(count):
        return lax.psum(values, axis_name)
    step = 1
    while step < count:
        values = values + lax.ppermute(values, axis_name, [(i, i ^ step) for i in range(count)])
        step *= 2
    return values


def gather_columns(values, axis_name):
    count = lax.axis_size(axis_name)
    index = lax.axis_index(axis_name)
    width = values.shape[1]
    whole = jnp.zeros((values.shape[0], width * count), values.dtype)
    whole = lax.dynamic_update_slice_in_dim(whole, values, index * width, axis=1)
    for shift in range(1, count):
        moved = lax.ppermute(values, axis_name, [(i, (i + shift) % count) for i in range(count)])
        source = lax.rem(index + count - shift, count)
        whole = lax.dynamic_update_slice_in_dim(whole, moved, source * width, axis=1)
    return whole


def spread_first(rows):
    place = lax.axis_index("shard")
    rows = jnp.where(place == 0, rows, lax.ppermute(rows, "shard", [(0, 2)]))
    rows = jnp.where(
        lax.rem(place, 2) == 1, lax.ppermute(rows, "shard", [(0, 1), (2, 3)]), rows
    )
    index = lax.axis_index(WIDE)
    blocks = {0: rows}
    for bit in (4, 2, 1):
        upper = (index & bit) != 0
        grown = {}
        for key, block in blocks.items():
            other = lax.ppermute(block, WIDE, [(i, i ^ bit) for i in range(8)])
            grown[key] = jnp.where(upper, other, block)
            grown[key | bit] = jnp.where(upper, block, other)
        blocks = grown
    return jnp.concatenate([blocks[key] for key in range(8)], axis=0)


owner_tree = {
    0: ([(3, 2), (1, 0)], [(2, 0)]),
    1: ([(0, 1), (3, 2)], [(2, 1)]),
    2: ([(3, 2), (0, 1)], [(1, 2)]),
    3: ([(0, 1), (2, 3)], [(1, 3)]),
}


def add_low(left, right):
    return (left.astype(jnp.float32) + right.astype(jnp.float32)).astype(left.dtype)


def tied(anchor, values):
    return lax.optimization_barrier((anchor, values))


def choose_owner(pieces):
    place = lax.axis_index("shard")
    own = pieces[0]
    for owner in range(1, len(pieces)):
        own = jnp.where(place == owner, pieces[owner], own)
    return own


def to_partner(values):
    return lax.ppermute(values, "core", [(0, 1), (1, 0)])


def paired(values):
    return jnp.concatenate([values, to_partner(values)], axis=0)


def split_rows(rows):
    return rows.reshape(rows.shape[0] // 16, 2, 8, rows.shape[1])


def one_parity(rows, parity):
    grouped = split_rows(rows)
    return lax.dynamic_index_in_dim(grouped, parity, axis=1, keepdims=False).reshape(
        rows.shape[0] // 2, rows.shape[1]
    )


def adam_rows(place, block, grad_low, state, carried):
    groups = block // 8

    def rows_of(i, place_ref):
        return (place_ref[0] + (i // 2) * place_ref[1], i % 2, 0, 0)

    spec = pl.BlockSpec((pl.Element(groups), pl.Element(1), pl.Element(8), pl.Element(D)), rows_of)

    def body(place_ref, grad_ref, param_ref, first_ref, second_ref, *rest):
        out_refs = rest[-4:]
        grad = grad_ref[...].astype(jnp.float32).reshape(groups, 1, 8, D)
        param_new, first_new, second_new = adam_update(
            param_ref[...], grad, first_ref[...], second_ref[...], weight_decay
        )
        for ref, value in zip(out_refs, (grad, param_new, first_new, second_new)):
            ref[...] = value

    count = grad_low.shape[0]
    shape = jax.ShapeDtypeStruct(state[0].shape, jnp.float32)
    return pl.pallas_call(
        body,
        grid_spec=pltpu.PrefetchScalarGridSpec(
            num_scalar_prefetch=1,
            grid=(count // block,),
            in_specs=[pl.BlockSpec((block, D), lambda i, place_ref: (i, 0))]
            + [spec] * 3
            + [pl.BlockSpec(memory_space=pl.ANY)] * len(carried),
            out_specs=[spec] * 4,
        ),
        out_shape=[shape] * 4,
        input_output_aliases={5 + k: k for k in range(len(carried))},
        cost_estimate=pl.CostEstimate(
            flops=20 * count * D, transcendentals=count * D, bytes_accessed=30 * count * D
        ),
        compiler_params=pltpu.CompilerParams(vmem_limit_bytes=56 * 2**20),
        name="adam_rows",
    )(place, grad_low, *state, *carried)


def per_device(
    tokens, seg_ids, cotangent, params, gains, first_moment, second_moment, gain_first, gain_second
):
    wide_count = wide_size()
    shard_count = lax.axis_size("shard")
    tree = wide_count == 8 and shard_count == 4
    owner_rows = params.shape[0]
    total_rows = owner_rows * shard_count
    early_rows = (HEADS + 2 * KV_HEADS) * HD + HEADS * HD
    wide_index = lax.axis_index(WIDE)
    core_index = lax.axis_index("core")

    def own_slice(first, count):
        part = count // wide_count
        return lax.dynamic_slice_in_dim(
            params, first + wide_index * part, part, axis=0
        ).astype(jnp.bfloat16)

    if tree:
        chip_rows = 2 * owner_rows // wide_count
        chip_slice = lax.dynamic_slice_in_dim(
            params, lax.axis_index("chip") * chip_rows, chip_rows, axis=0
        )
        rows_used = lax.all_gather(
            one_parity(chip_slice, core_index).astype(jnp.bfloat16),
            ("shard", "chip"),
            axis=0,
            tiled=True,
        )
        early_used = spread_first(own_slice(0, early_rows))
        split = 2
    else:
        rows_used = lax.all_gather(
            own_slice(0, owner_rows), ("shard",) + WIDE, axis=0, tiled=True
        )
        early_used = rows_used[:early_rows]
        split = 1
    gains_used = gather_columns(gains.astype(jnp.bfloat16), "shard")
    gains_float = gains_used.astype(jnp.float32)
    query_width = HEADS * HD
    kv_width = KV_HEADS * HD
    per_group = HEADS // KV_HEADS
    qkv_rows = query_width + 2 * kv_width
    out_end = qkv_rows + query_width
    gate_end = out_end + 2 * FF
    w_qkv = early_used[:qkv_rows]
    w_out = early_used[qkv_rows:out_end]
    gate_first, up_first, down_first, hidden_width = (
        out_end // split,
        (out_end + FF) // split,
        gate_end // split,
        FF // split,
    )
    w_gate_up = rows_used[gate_first:down_first]
    w_down = rows_used[down_first:]
    row_count = tokens.shape[0]
    block_rows = min(512, row_count)
    block_count = row_count // block_rows
    query_scale = HD ** (-0.5)
    inputs = tokens.astype(jnp.float32)
    cosine_table, sine_table = rotary_tables(positions_of(seg_ids), HD)
    normed, pull_first = jax.vjp(rms_scale, inputs, gains_float[0])
    normed_low = normed.astype(jnp.bfloat16)
    projected = times_transposed(normed_low, w_qkv)
    query_raw = projected[:, :query_width].reshape(row_count, HEADS, HD)
    key_raw = projected[:, query_width : query_width + kv_width].reshape(row_count, KV_HEADS, HD)
    value_heads = (
        projected[:, query_width + kv_width :].astype(jnp.bfloat16).reshape(row_count, KV_HEADS, HD)
    )
    queries = (rotate(query_raw, cosine_table, sine_table) * query_scale).astype(jnp.bfloat16)
    key_heads = rotate(key_raw, cosine_table, sine_table).astype(jnp.bfloat16)
    query_blocks = queries.reshape(block_count, block_rows, KV_HEADS, per_group, HD)
    segment_blocks = seg_ids.reshape(block_count, block_rows)
    block_starts = jnp.arange(block_count, dtype=jnp.int32) * block_rows

    def forward_block(inputs_block):
        query_block, segment_block, first_row = inputs_block
        scores = jnp.einsum(
            "qgnd,kgd->gnqk", query_block, key_heads, preferred_element_type=jnp.float32
        )
        capped = softcap_limit * jnp.tanh(scores / softcap_limit)
        allowed = block_mask(segment_block, seg_ids, first_row)
        row_top = jnp.max(jnp.where(allowed, capped, masked_floor), axis=-1, keepdims=True)
        weights_exp = jnp.where(allowed, jnp.exp(jnp.where(allowed, capped - row_top, 0.0)), 0.0)
        totals = jnp.sum(weights_exp, axis=-1, keepdims=True)
        probability = (weights_exp / totals).astype(jnp.bfloat16)
        mixed_block = jnp.einsum(
            "gnqk,kgd->qgnd", probability, value_heads, preferred_element_type=jnp.float32
        )
        return (mixed_block, row_top + jnp.log(totals))

    mixed_heads, log_totals = lax.map(forward_block, (query_blocks, segment_blocks, block_starts))
    mixed_low = mixed_heads.reshape(row_count, query_width).astype(jnp.bfloat16)
    attended = jnp.dot(mixed_low, w_out, preferred_element_type=jnp.float32)
    attn_normed, pull_second = jax.vjp(rms_scale, attended, gains_float[1])
    first_sum = inputs + attn_normed
    ffn_input, pull_third = jax.vjp(rms_scale, first_sum, gains_float[2])
    ffn_low = ffn_input.astype(jnp.bfloat16)
    if tree:
        ffn_low = paired(ffn_low)
    gate_up = times_transposed(ffn_low, w_gate_up)
    hidden, pull_fourth = jax.vjp(geglu, gate_up[:, :hidden_width], gate_up[:, hidden_width:])
    hidden_low = hidden.astype(jnp.bfloat16)
    if tree:
        other_branch = jnp.dot(
            hidden_low[row_count:], w_down, preferred_element_type=jnp.float32
        )
        hidden_low, other_branch = tied(hidden_low, other_branch)
        own_branch, other_branch = tied(
            jnp.dot(hidden_low[:row_count], w_down, preferred_element_type=jnp.float32),
            to_partner(other_branch),
        )
        branch = own_branch + other_branch
    else:
        branch = jnp.dot(hidden_low, w_down, preferred_element_type=jnp.float32)
    ffn_normed, pull_fifth = jax.vjp(rms_scale, branch, gains_float[3])
    result = first_sum + ffn_normed
    upstream = cotangent.astype(jnp.float32)
    branch_grad, gain_four = pull_fifth(upstream)
    branch_low = branch_grad.astype(jnp.bfloat16)
    if tree:
        branch_low = paired(branch_low)

    def product_rows(left, right):
        def rows(first, last):
            return contract_rows(left[:, first:last], right).astype(jnp.bfloat16)

        return rows

    factors = {
        "down": (down_first, total_rows // split, product_rows(hidden_low, branch_low))
    }
    steps = {}
    late_rows = qkv_rows // split
    segment_rows = owner_rows // split

    def bounds(key):
        return (max(key * segment_rows, late_rows), (key + 1) * segment_rows)

    def plane_terms(first, last):
        parts = [
            rows(max(first, start) - start, min(last, end) - start)
            for start, end, rows in sorted(factors.values(), key=lambda f: f[0])
            if max(first, start) < min(last, end)
        ]
        return parts[0] if len(parts) == 1 else jnp.concatenate(parts, axis=0)

    def start_ready(anchor, lowest):
        keys = [
            key
            for key in reversed(range(shard_count))
            if key not in steps and bounds(key)[0] >= lowest
        ]
        if not tree or not keys:
            return anchor
        terms = [plane_terms(*bounds(key)) for key in keys]
        for key, term in zip(keys, terms):
            steps[key] = [lax.psum_scatter(term, "chip", scatter_dimension=0, tiled=True)]
        return tied(anchor, terms)[0]

    def advance(key):
        pairs = owner_tree[max(key, 0)][len(steps[key]) - 1]
        held = steps[key][-1]
        steps[key].append(add_low(held, lax.ppermute(held, "shard", pairs)))

    def tick(anchor, *keys):
        if not tree:
            return anchor
        anchor, values = tied(anchor, [steps[key][-1] for key in keys])
        for key, value in zip(keys, values):
            steps[key][-1] = value
            advance(key)
        return anchor

    branch_low = start_ready(branch_low, down_first)
    hidden_grad = times_transposed(branch_low, w_down)
    gate_grad, up_grad = pull_fourth(hidden_grad)
    gate_low, up_low = gate_grad.astype(jnp.bfloat16), up_grad.astype(jnp.bfloat16)
    factors["gate"] = (gate_first, up_first, product_rows(gate_low, ffn_low))
    factors["up"] = (up_first, down_first, product_rows(up_low, ffn_low))
    gate_low, up_low = start_ready((gate_low, up_low), gate_first)
    gate_low, up_low = tick((gate_low, up_low), 3)

    def input_grad_of(first, last):
        return jnp.dot(
            gate_low[first:last], w_gate_up[:hidden_width], preferred_element_type=jnp.float32
        ) + jnp.dot(
            up_low[first:last], w_gate_up[hidden_width:], preferred_element_type=jnp.float32
        )

    if tree:
        other_grad = input_grad_of(row_count, 2 * row_count)
        (gate_low, up_low), other_grad = tied((gate_low, up_low), other_grad)
        ffn_input_grad = input_grad_of(0, row_count) + to_partner(other_grad)
    else:
        ffn_input_grad = input_grad_of(0, row_count)
    ffn_input_grad = tick(ffn_input_grad, 3)
    sum_grad_part, gain_three = pull_third(ffn_input_grad)
    sum_grad = upstream + sum_grad_part
    attended_grad, gain_two = pull_second(sum_grad)
    attended_low = attended_grad.astype(jnp.bfloat16)
    out_rows = product_rows(mixed_low, attended_low)

    def summed_out_rows(first, last):
        rows = out_rows(first * 2, last * 2)
        other = to_partner(one_parity(rows, 1 - core_index))
        return add_low(one_parity(rows, core_index), other)

    factors["out"] = (
        qkv_rows // split,
        gate_first,
        summed_out_rows if tree else out_rows,
    )
    mixed_grad = (
        times_transposed(attended_low, w_out)
        .astype(jnp.bfloat16)
        .reshape(block_count, block_rows, KV_HEADS, per_group, HD)
    )

    mixed_grad = start_ready(mixed_grad, late_rows)
    mixed_grad = tick(mixed_grad, 2)

    def backward_block(running, inputs_block):
        key_acc, value_acc = running
        query_block, grad_block, segment_block, first_row, log_block = inputs_block
        scores = jnp.einsum(
            "qgnd,kgd->gnqk", query_block, key_heads, preferred_element_type=jnp.float32
        )
        capped = softcap_limit * jnp.tanh(scores / softcap_limit)
        allowed = block_mask(segment_block, seg_ids, first_row)
        probability = jnp.where(allowed, jnp.exp(jnp.where(allowed, capped - log_block, 0.0)), 0.0)
        probability_low = probability.astype(jnp.bfloat16)
        value_acc = value_acc + jnp.einsum(
            "gnqk,qgnd->kgd", probability_low, grad_block, preferred_element_type=jnp.float32
        )
        prob_grad = jnp.einsum(
            "qgnd,kgd->gnqk", grad_block, value_heads, preferred_element_type=jnp.float32
        )
        centred = jnp.sum(probability * prob_grad, axis=-1, keepdims=True)
        score_grad = (
            probability * (prob_grad - centred) * (1.0 - (capped / softcap_limit) ** 2)
        ).astype(jnp.bfloat16)
        query_grad_block = jnp.einsum(
            "gnqk,kgd->qgnd", score_grad, key_heads, preferred_element_type=jnp.float32
        )
        key_acc = key_acc + jnp.einsum(
            "gnqk,qgnd->kgd", score_grad, query_block, preferred_element_type=jnp.float32
        )
        return ((key_acc, value_acc), query_grad_block)

    zero_heads = jnp.zeros((row_count, KV_HEADS, HD), jnp.float32)
    (key_grad, value_grad), query_grad = lax.scan(
        backward_block,
        (zero_heads, zero_heads),
        (query_blocks, mixed_grad, segment_blocks, block_starts, log_totals),
    )
    query_grad = tick(query_grad, 2, 1)
    query_raw_grad = rotate(
        query_grad.reshape(row_count, HEADS, HD) * query_scale, cosine_table, -sine_table
    )
    key_raw_grad = rotate(key_grad, cosine_table, -sine_table)
    qkv_low = jnp.concatenate(
        [
            query_raw_grad.reshape(row_count, query_width),
            key_raw_grad.reshape(row_count, kv_width),
            value_grad.reshape(row_count, kv_width),
        ],
        axis=1,
    ).astype(jnp.bfloat16)
    factors["qkv"] = (0, qkv_rows // split, product_rows(qkv_low, normed_low))
    normed_grad = jnp.dot(qkv_low, w_qkv, preferred_element_type=jnp.float32)
    input_part, gain_one = pull_first(normed_grad)
    input_grad = sum_grad + input_part
    state = (params, first_moment, second_moment)
    if tree:
        qkv_grad = product_rows(qkv_low, normed_low)(0, qkv_rows)
        by_piece = (
            qkv_grad.reshape(wide_count // 2, -1, 2, 8, D)
            .transpose(0, 2, 1, 3, 4)
            .reshape(qkv_rows, D)
        )
        steps[-1] = [lax.psum_scatter(by_piece, WIDE, scatter_dimension=0, tiled=True)]
        for key in (3, 2, 1, 0, -1):
            while len(steps[key]) < 3:
                advance(key)
        late_part = qkv_rows // wide_count
        early_part = owner_rows // wide_count - late_part
        whole_pieces = [steps[owner][-1] for owner in range(1, shard_count)]
        early_piece = choose_owner([steps[0][-1]] + [p[:early_part] for p in whole_pieces])
        late_piece = choose_owner([steps[-1][-1]] + [p[early_part:] for p in whole_pieces])
        first_owner = lax.axis_index("shard") == 0
        early_groups, late_groups = early_part // 8, late_part // 8
        early_place = jnp.where(
            first_owner,
            jnp.array([qkv_rows // 16, early_groups], jnp.int32),
            jnp.array([0, early_groups + late_groups], jnp.int32),
        )
        late_place = jnp.where(
            first_owner,
            jnp.array([0, late_groups], jnp.int32),
            jnp.array([early_groups, early_groups + late_groups], jnp.int32),
        )
        early_low = lax.all_gather(early_piece, WIDE, axis=0, tiled=True)
        late_low = lax.all_gather(late_piece, WIDE, axis=0, tiled=True)
        state = [split_rows(rows) for rows in (params, first_moment, second_moment)]
        carried = adam_rows(early_place, early_part, early_low, state, ())
        row_grad, new_params, new_first, new_second = [
            rows.reshape(owner_rows, D)
            for rows in adam_rows(late_place, late_part, late_low, state, carried)
        ]
    else:
        own = lax.psum_scatter(
            plane_terms(0, total_rows), ("shard",) + WIDE, scatter_dimension=0, tiled=True
        )
        row_grad = lax.all_gather(own, WIDE, axis=0, tiled=True).astype(jnp.float32)
        new_params, new_first, new_second = adam_update(
            params, row_grad, first_moment, second_moment, weight_decay
        )
    gain_terms = jnp.stack([gain_one, gain_two, gain_three, gain_four])
    gain_total = butterfly_sum(
        butterfly_sum(gain_terms, WIDE, wide_count), "shard", shard_count
    )
    gain_grad = lax.dynamic_slice_in_dim(
        gain_total, lax.axis_index("shard") * gains.shape[1], gains.shape[1], axis=1
    )
    new_gains, new_gain_first, new_gain_second = adam_update(
        gains, gain_grad, gain_first, gain_second, 0.0
    )
    return (
        result.astype(jnp.bfloat16),
        input_grad.astype(jnp.bfloat16),
        row_grad,
        gain_grad,
        new_params,
        new_gains,
        new_first,
        new_second,
        new_gain_first,
        new_gain_second,
    )


def solution(mesh):
    split_mesh = Mesh(
        mesh.devices.reshape(mesh.shape["wide"] // 2, 2, mesh.shape["shard"]),
        ("chip", "core", "shard"),
    )
    return jax.shard_map(
        per_device,
        mesh=split_mesh,
        in_specs=(
            P(("chip", "core", "shard"), None),
            P(("chip", "core", "shard")),
            P(("chip", "core", "shard"), None),
            P("shard", None),
            P(None, "shard"),
            P("shard", None),
            P("shard", None),
            P(None, "shard"),
            P(None, "shard"),
        ),
        out_specs=(
            P(("chip", "core", "shard"), None),
            P(("chip", "core", "shard"), None),
            P("shard", None),
            P(None, "shard"),
            P("shard", None),
            P(None, "shard"),
            P("shard", None),
            P("shard", None),
            P(None, "shard"),
            P(None, "shard"),
        ),
        check_vma=False,
    )
```

```python
import jax
import jax.numpy as jnp
from jax import lax
from jax.experimental import pallas as pl
from jax.experimental.pallas import tpu as pltpu
from jax.sharding import Mesh
from jax.sharding import PartitionSpec as P


D = 1152
FF = 6912
HEADS = 4
KV_HEADS = 1
HD = 256
WINDOW = 512


norm_epsilon = 1e-06
softcap_limit = 50.0
rope_base = 10000.0
beta_first = 0.9
beta_second = 0.95
learn_rate = 0.02
adam_epsilon = 1e-08
weight_decay = 0.1
adam_step = 10.0
masked_floor = -1e30


def rms_scale(values, gain_row):
    return (
        values
        * lax.rsqrt(jnp.mean(values * values, axis=-1, keepdims=True) + norm_epsilon)
        * (1.0 + gain_row)
    )


def positions_of(segments):
    index_row = jnp.arange(segments.shape[0], dtype=jnp.int32)
    previous = jnp.concatenate([segments[:1] - 1, segments[:-1]])
    first_slot = lax.cummax(jnp.where(segments != previous, index_row, 0), axis=0)
    return index_row - first_slot


def rotary_tables(positions, head_width):
    half_width = head_width // 2
    frequency = rope_base ** (-2.0 * jnp.arange(half_width, dtype=jnp.float32) / head_width)
    angles = positions.astype(jnp.float32)[:, None] * frequency[None, :]
    return (jnp.cos(angles), jnp.sin(angles))


def rotate(values, cosine_table, sine_table):
    half_width = values.shape[-1] // 2
    first_half = values[..., :half_width]
    second_half = values[..., half_width:]
    cosine_part = cosine_table[:, None, :]
    sine_part = sine_table[:, None, :]
    return jnp.concatenate(
        [
            first_half * cosine_part - second_half * sine_part,
            second_half * cosine_part + first_half * sine_part,
        ],
        axis=-1,
    )


def geglu(gate_value, up_value):
    return jax.nn.gelu(gate_value, approximate=True) * up_value


def contract_rows(left_side, right_side):
    return lax.dot_general(
        left_side, right_side, (((0,), (0,)), ((), ())), preferred_element_type=jnp.float32
    )


def times_transposed(left_side, right_side):
    return lax.dot_general(
        left_side, right_side, (((1,), (1,)), ((), ())), preferred_element_type=jnp.float32
    )


def block_mask(query_segments, key_segments, first_row):
    query_index = first_row + jnp.arange(query_segments.shape[0], dtype=jnp.int32)
    key_index = jnp.arange(key_segments.shape[0], dtype=jnp.int32)
    return (
        (query_segments[:, None] == key_segments[None, :])
        & (key_index[None, :] <= query_index[:, None])
        & (query_index[:, None] - key_index[None, :] < WINDOW)
    )


def adam_update(param_old, grad_sum, first_old, second_old, decay_rate):
    first_new = beta_first * first_old + (1.0 - beta_first) * grad_sum
    second_new = beta_second * second_old + (1.0 - beta_second) * grad_sum * grad_sum
    corrected = (
        first_new
        / (1.0 - beta_first**adam_step)
        / (jnp.sqrt(second_new / (1.0 - beta_second**adam_step)) + adam_epsilon)
    )
    return (param_old - learn_rate * (corrected + decay_rate * param_old), first_new, second_new)


def power_of_two(count):
    return count & (count - 1) == 0


WIDE = ("chip", "core")


def wide_size():
    return lax.axis_size("chip") * lax.axis_size("core")


def butterfly_sum(values, axis_name, count):
    if not power_of_two(count):
        return lax.psum(values, axis_name)
    step = 1
    while step < count:
        values = values + lax.ppermute(values, axis_name, [(i, i ^ step) for i in range(count)])
        step *= 2
    return values


def gather_columns(values, axis_name):
    count = lax.axis_size(axis_name)
    index = lax.axis_index(axis_name)
    width = values.shape[1]
    whole = jnp.zeros((values.shape[0], width * count), values.dtype)
    whole = lax.dynamic_update_slice_in_dim(whole, values, index * width, axis=1)
    for shift in range(1, count):
        moved = lax.ppermute(values, axis_name, [(i, (i + shift) % count) for i in range(count)])
        source = lax.rem(index + count - shift, count)
        whole = lax.dynamic_update_slice_in_dim(whole, moved, source * width, axis=1)
    return whole


def spread_first(rows):
    place = lax.axis_index("shard")
    rows = jnp.where(place == 0, rows, lax.ppermute(rows, "shard", [(0, 2)]))
    rows = jnp.where(
        lax.rem(place, 2) == 1, lax.ppermute(rows, "shard", [(0, 1), (2, 3)]), rows
    )
    index = lax.axis_index(WIDE)
    blocks = {0: rows}
    for bit in (4, 2, 1):
        upper = (index & bit) != 0
        grown = {}
        for key, block in blocks.items():
            other = lax.ppermute(block, WIDE, [(i, i ^ bit) for i in range(8)])
            grown[key] = jnp.where(upper, other, block)
            grown[key | bit] = jnp.where(upper, block, other)
        blocks = grown
    return jnp.concatenate([blocks[key] for key in range(8)], axis=0)


owner_tree = {
    0: ([(3, 2), (1, 0)], [(2, 0)]),
    1: ([(0, 1), (3, 2)], [(2, 1)]),
    2: ([(3, 2), (0, 1)], [(1, 2)]),
    3: ([(0, 1), (2, 3)], [(1, 3)]),
}


def add_low(left, right):
    return (left.astype(jnp.float32) + right.astype(jnp.float32)).astype(left.dtype)


def tied(anchor, values):
    return lax.optimization_barrier((anchor, values))


def choose_owner(pieces):
    place = lax.axis_index("shard")
    own = pieces[0]
    for owner in range(1, len(pieces)):
        own = jnp.where(place == owner, pieces[owner], own)
    return own


def to_partner(values):
    return lax.ppermute(values, "core", [(0, 1), (1, 0)])


def paired(values):
    return jnp.concatenate([values, to_partner(values)], axis=0)


def split_rows(rows):
    return rows.reshape(rows.shape[0] // 16, 2, 8, rows.shape[1])


def one_parity(rows, parity):
    grouped = split_rows(rows)
    return lax.dynamic_index_in_dim(grouped, parity, axis=1, keepdims=False).reshape(
        rows.shape[0] // 2, rows.shape[1]
    )


def adam_rows(place, block, grad_low, state, carried):
    groups = block // 8

    def rows_of(i, place_ref):
        return (place_ref[0] + (i // 2) * place_ref[1], i % 2, 0, 0)

    spec = pl.BlockSpec((pl.Element(groups), pl.Element(1), pl.Element(8), pl.Element(D)), rows_of)

    def body(place_ref, grad_ref, param_ref, first_ref, second_ref, *rest):
        out_refs = rest[-4:]
        grad = grad_ref[...].astype(jnp.float32).reshape(groups, 1, 8, D)
        param_new, first_new, second_new = adam_update(
            param_ref[...], grad, first_ref[...], second_ref[...], weight_decay
        )
        for ref, value in zip(out_refs, (grad, param_new, first_new, second_new)):
            ref[...] = value

    count = grad_low.shape[0]
    shape = jax.ShapeDtypeStruct(state[0].shape, jnp.float32)
    return pl.pallas_call(
        body,
        grid_spec=pltpu.PrefetchScalarGridSpec(
            num_scalar_prefetch=1,
            grid=(count // block,),
            in_specs=[pl.BlockSpec((block, D), lambda i, place_ref: (i, 0))]
            + [spec] * 3
            + [pl.BlockSpec(memory_space=pl.ANY)] * len(carried),
            out_specs=[spec] * 4,
        ),
        out_shape=[shape] * 4,
        input_output_aliases={5 + k: k for k in range(len(carried))},
        cost_estimate=pl.CostEstimate(
            flops=20 * count * D, transcendentals=count * D, bytes_accessed=30 * count * D
        ),
        compiler_params=pltpu.CompilerParams(vmem_limit_bytes=56 * 2**20),
        name="adam_rows",
    )(place, grad_low, *state, *carried)


def per_device(
    tokens, seg_ids, cotangent, params, gains, first_moment, second_moment, gain_first, gain_second
):
    wide_count = wide_size()
    shard_count = lax.axis_size("shard")
    tree = wide_count == 8 and shard_count == 4
    owner_rows = params.shape[0]
    total_rows = owner_rows * shard_count
    early_rows = (HEADS + 2 * KV_HEADS) * HD + HEADS * HD
    wide_index = lax.axis_index(WIDE)
    core_index = lax.axis_index("core")

    def own_slice(first, count):
        part = count // wide_count
        return lax.dynamic_slice_in_dim(
            params, first + wide_index * part, part, axis=0
        ).astype(jnp.bfloat16)

    if tree:
        chip_rows = 2 * owner_rows // wide_count
        chip_slice = lax.dynamic_slice_in_dim(
            params, lax.axis_index("chip") * chip_rows, chip_rows, axis=0
        )
        rows_used = lax.all_gather(
            one_parity(chip_slice, core_index).astype(jnp.bfloat16),
            ("shard", "chip"),
            axis=0,
            tiled=True,
        )
        early_used = spread_first(own_slice(0, early_rows))
        split = 2
    else:
        rows_used = lax.all_gather(
            own_slice(0, owner_rows), ("shard",) + WIDE, axis=0, tiled=True
        )
        early_used = rows_used[:early_rows]
        split = 1
    gains_used = gather_columns(gains.astype(jnp.bfloat16), "shard")
    gains_float = gains_used.astype(jnp.float32)
    query_width = HEADS * HD
    kv_width = KV_HEADS * HD
    per_group = HEADS // KV_HEADS
    qkv_rows = query_width + 2 * kv_width
    out_end = qkv_rows + query_width
    gate_end = out_end + 2 * FF
    w_qkv = early_used[:qkv_rows]
    w_out = early_used[qkv_rows:out_end]
    gate_first, up_first, down_first, hidden_width = (
        out_end // split,
        (out_end + FF) // split,
        gate_end // split,
        FF // split,
    )
    w_gate_up = rows_used[gate_first:down_first]
    w_down = rows_used[down_first:]
    row_count = tokens.shape[0]
    block_rows = min(512, row_count)
    block_count = row_count // block_rows
    query_scale = HD ** (-0.5)
    inputs = tokens.astype(jnp.float32)
    cosine_table, sine_table = rotary_tables(positions_of(seg_ids), HD)
    normed, pull_first = jax.vjp(rms_scale, inputs, gains_float[0])
    normed_low = normed.astype(jnp.bfloat16)
    projected = times_transposed(normed_low, w_qkv)
    query_raw = projected[:, :query_width].reshape(row_count, HEADS, HD)
    key_raw = projected[:, query_width : query_width + kv_width].reshape(row_count, KV_HEADS, HD)
    value_heads = (
        projected[:, query_width + kv_width :].astype(jnp.bfloat16).reshape(row_count, KV_HEADS, HD)
    )
    queries = (rotate(query_raw, cosine_table, sine_table) * query_scale).astype(jnp.bfloat16)
    key_heads = rotate(key_raw, cosine_table, sine_table).astype(jnp.bfloat16)
    query_blocks = queries.reshape(block_count, block_rows, KV_HEADS, per_group, HD)
    segment_blocks = seg_ids.reshape(block_count, block_rows)
    block_starts = jnp.arange(block_count, dtype=jnp.int32) * block_rows

    def forward_block(inputs_block):
        query_block, segment_block, first_row = inputs_block
        scores = jnp.einsum(
            "qgnd,kgd->gnqk", query_block, key_heads, preferred_element_type=jnp.float32
        )
        capped = softcap_limit * jnp.tanh(scores / softcap_limit)
        allowed = block_mask(segment_block, seg_ids, first_row)
        row_top = jnp.max(jnp.where(allowed, capped, masked_floor), axis=-1, keepdims=True)
        weights_exp = jnp.where(allowed, jnp.exp(jnp.where(allowed, capped - row_top, 0.0)), 0.0)
        totals = jnp.sum(weights_exp, axis=-1, keepdims=True)
        probability = (weights_exp / totals).astype(jnp.bfloat16)
        mixed_block = jnp.einsum(
            "gnqk,kgd->qgnd", probability, value_heads, preferred_element_type=jnp.float32
        )
        return (mixed_block, row_top + jnp.log(totals))

    mixed_heads, log_totals = lax.map(forward_block, (query_blocks, segment_blocks, block_starts))
    mixed_low = mixed_heads.reshape(row_count, query_width).astype(jnp.bfloat16)
    attended = jnp.dot(mixed_low, w_out, preferred_element_type=jnp.float32)
    attn_normed, pull_second = jax.vjp(rms_scale, attended, gains_float[1])
    first_sum = inputs + attn_normed
    ffn_input, pull_third = jax.vjp(rms_scale, first_sum, gains_float[2])
    ffn_low = ffn_input.astype(jnp.bfloat16)
    if tree:
        ffn_low = paired(ffn_low)
    gate_up_kept = lax.optimization_barrier(
        times_transposed(ffn_low, w_gate_up).astype(jnp.bfloat16)
    )

    def both_wide(gate_up):
        return (
            gate_up[:, :hidden_width].astype(jnp.float32),
            gate_up[:, hidden_width:].astype(jnp.float32),
        )

    hidden = geglu(*both_wide(gate_up_kept))
    hidden_low = hidden.astype(jnp.bfloat16)
    if tree:
        other_branch = jnp.dot(
            hidden_low[row_count:], w_down, preferred_element_type=jnp.float32
        )
        hidden_low, other_branch = tied(hidden_low, other_branch)
        own_branch, other_branch = tied(
            jnp.dot(hidden_low[:row_count], w_down, preferred_element_type=jnp.float32),
            to_partner(other_branch),
        )
        branch = own_branch + other_branch
    else:
        branch = jnp.dot(hidden_low, w_down, preferred_element_type=jnp.float32)
    ffn_normed, pull_fifth = jax.vjp(rms_scale, branch, gains_float[3])
    result = first_sum + ffn_normed
    upstream = cotangent.astype(jnp.float32)
    branch_grad, gain_four = pull_fifth(upstream)
    branch_low = branch_grad.astype(jnp.bfloat16)
    if tree:
        branch_low = paired(branch_low)

    def product_rows(left, right):
        def rows(first, last):
            return contract_rows(left[:, first:last], right).astype(jnp.bfloat16)

        return rows

    factors = {
        "down": (down_first, total_rows // split, product_rows(hidden_low, branch_low))
    }
    steps = {}
    late_rows = qkv_rows // split
    segment_rows = owner_rows // split

    def bounds(key):
        return (max(key * segment_rows, late_rows), (key + 1) * segment_rows)

    def plane_terms(first, last):
        parts = [
            rows(max(first, start) - start, min(last, end) - start)
            for start, end, rows in sorted(factors.values(), key=lambda f: f[0])
            if max(first, start) < min(last, end)
        ]
        return parts[0] if len(parts) == 1 else jnp.concatenate(parts, axis=0)

    def start_ready(anchor, lowest):
        keys = [
            key
            for key in reversed(range(shard_count))
            if key not in steps and bounds(key)[0] >= lowest
        ]
        if not tree or not keys:
            return anchor
        terms = [plane_terms(*bounds(key)) for key in keys]
        for key, term in zip(keys, terms):
            steps[key] = [lax.psum_scatter(term, "chip", scatter_dimension=0, tiled=True)]
        return tied(anchor, terms)[0]

    def advance(key):
        pairs = owner_tree[max(key, 0)][len(steps[key]) - 1]
        held = steps[key][-1]
        moved = lax.ppermute(held, "shard", pairs)
        steps[key].append(add_low(held, moved))

    def tick(anchor, *keys):
        if not tree:
            return anchor
        anchor, values = tied(anchor, [steps[key][-1] for key in keys])
        for key, value in zip(keys, values):
            steps[key][-1] = value
            advance(key)
        return anchor

    branch_low = start_ready(branch_low, down_first)
    hidden_grad = times_transposed(branch_low, w_down)
    gate_up_again, branch_low = tied(gate_up_kept, branch_low)
    _, pull_fourth = jax.vjp(geglu, *both_wide(gate_up_again))
    gate_grad, up_grad = pull_fourth(hidden_grad)
    gate_low, up_low = gate_grad.astype(jnp.bfloat16), up_grad.astype(jnp.bfloat16)
    factors["gate"] = (gate_first, up_first, product_rows(gate_low, ffn_low))
    factors["up"] = (up_first, down_first, product_rows(up_low, ffn_low))
    gate_low, up_low = start_ready((gate_low, up_low), gate_first)
    gate_low, up_low = tick((gate_low, up_low), 3)

    def input_grad_of(first, last):
        return jnp.dot(
            gate_low[first:last], w_gate_up[:hidden_width], preferred_element_type=jnp.float32
        ) + jnp.dot(
            up_low[first:last], w_gate_up[hidden_width:], preferred_element_type=jnp.float32
        )

    if tree:
        other_grad = input_grad_of(row_count, 2 * row_count)
        (gate_low, up_low), other_grad = tied((gate_low, up_low), other_grad)
        ffn_input_grad = input_grad_of(0, row_count) + to_partner(other_grad)
    else:
        ffn_input_grad = input_grad_of(0, row_count)
    ffn_input_grad = tick(ffn_input_grad, 2)
    sum_grad_part, gain_three = pull_third(ffn_input_grad)
    sum_grad = upstream + sum_grad_part
    attended_grad, gain_two = pull_second(sum_grad)
    attended_low = attended_grad.astype(jnp.bfloat16)
    out_rows = product_rows(mixed_low, attended_low)

    def summed_out_rows(first, last):
        rows = out_rows(first * 2, last * 2)
        other = to_partner(one_parity(rows, 1 - core_index))
        return add_low(one_parity(rows, core_index), other)

    factors["out"] = (
        qkv_rows // split,
        gate_first,
        summed_out_rows if tree else out_rows,
    )
    mixed_grad = (
        times_transposed(attended_low, w_out)
        .astype(jnp.bfloat16)
        .reshape(block_count, block_rows, KV_HEADS, per_group, HD)
    )

    mixed_grad = start_ready(mixed_grad, late_rows)
    mixed_grad = tick(mixed_grad, 3, 1)

    def backward_block(running, inputs_block):
        key_acc, value_acc = running
        query_block, grad_block, segment_block, first_row, log_block = inputs_block
        scores = jnp.einsum(
            "qgnd,kgd->gnqk", query_block, key_heads, preferred_element_type=jnp.float32
        )
        capped = softcap_limit * jnp.tanh(scores / softcap_limit)
        allowed = block_mask(segment_block, seg_ids, first_row)
        probability = jnp.where(allowed, jnp.exp(jnp.where(allowed, capped - log_block, 0.0)), 0.0)
        probability_low = probability.astype(jnp.bfloat16)
        value_acc = value_acc + jnp.einsum(
            "gnqk,qgnd->kgd", probability_low, grad_block, preferred_element_type=jnp.float32
        )
        prob_grad = jnp.einsum(
            "qgnd,kgd->gnqk", grad_block, value_heads, preferred_element_type=jnp.float32
        )
        centred = jnp.sum(probability * prob_grad, axis=-1, keepdims=True)
        score_grad = (
            probability * (prob_grad - centred) * (1.0 - (capped / softcap_limit) ** 2)
        ).astype(jnp.bfloat16)
        query_grad_block = jnp.einsum(
            "gnqk,kgd->qgnd", score_grad, key_heads, preferred_element_type=jnp.float32
        )
        key_acc = key_acc + jnp.einsum(
            "gnqk,qgnd->kgd", score_grad, query_block, preferred_element_type=jnp.float32
        )
        return ((key_acc, value_acc), query_grad_block)

    zero_heads = jnp.zeros((row_count, KV_HEADS, HD), jnp.float32)
    (key_grad, value_grad), query_grad = lax.scan(
        backward_block,
        (zero_heads, zero_heads),
        (query_blocks, mixed_grad, segment_blocks, block_starts, log_totals),
    )
    query_grad = tick(query_grad, 2, 1, 0)
    query_raw_grad = rotate(
        query_grad.reshape(row_count, HEADS, HD) * query_scale, cosine_table, -sine_table
    )
    key_raw_grad = rotate(key_grad, cosine_table, -sine_table)
    qkv_low = jnp.concatenate(
        [
            query_raw_grad.reshape(row_count, query_width),
            key_raw_grad.reshape(row_count, kv_width),
            value_grad.reshape(row_count, kv_width),
        ],
        axis=1,
    ).astype(jnp.bfloat16)
    factors["qkv"] = (0, qkv_rows // split, product_rows(qkv_low, normed_low))
    normed_grad = jnp.dot(qkv_low, w_qkv, preferred_element_type=jnp.float32)
    input_part, gain_one = pull_first(normed_grad)
    input_grad = sum_grad + input_part
    state = (params, first_moment, second_moment)
    if tree:
        qkv_grad = product_rows(qkv_low, normed_low)(0, qkv_rows)
        qkv_grad = tick(qkv_grad, 0)
        by_piece = (
            qkv_grad.reshape(wide_count // 2, -1, 2, 8, D)
            .transpose(0, 2, 1, 3, 4)
            .reshape(qkv_rows, D)
        )
        steps[-1] = [lax.psum_scatter(by_piece, WIDE, scatter_dimension=0, tiled=True)]
        for key in (3, 2, 1, 0, -1):
            while len(steps[key]) < 3:
                advance(key)
        late_part = qkv_rows // wide_count
        early_part = owner_rows // wide_count - late_part
        whole_pieces = [steps[owner][-1] for owner in range(1, shard_count)]
        early_piece = choose_owner([steps[0][-1]] + [p[:early_part] for p in whole_pieces])
        late_piece = choose_owner([steps[-1][-1]] + [p[early_part:] for p in whole_pieces])
        first_owner = lax.axis_index("shard") == 0
        early_groups, late_groups = early_part // 8, late_part // 8
        early_place = jnp.where(
            first_owner,
            jnp.array([qkv_rows // 16, early_groups], jnp.int32),
            jnp.array([0, early_groups + late_groups], jnp.int32),
        )
        late_place = jnp.where(
            first_owner,
            jnp.array([0, late_groups], jnp.int32),
            jnp.array([early_groups, early_groups + late_groups], jnp.int32),
        )
        early_low = lax.all_gather(early_piece, WIDE, axis=0, tiled=True)
        late_low = lax.all_gather(late_piece, WIDE, axis=0, tiled=True)
        state = [split_rows(rows) for rows in (params, first_moment, second_moment)]
        carried = adam_rows(early_place, early_part, early_low, state, ())
        row_grad, new_params, new_first, new_second = [
            rows.reshape(owner_rows, D)
            for rows in adam_rows(late_place, late_part, late_low, state, carried)
        ]
    else:
        own = lax.psum_scatter(
            plane_terms(0, total_rows), ("shard",) + WIDE, scatter_dimension=0, tiled=True
        )
        row_grad = lax.all_gather(own, WIDE, axis=0, tiled=True).astype(jnp.float32)
        new_params, new_first, new_second = adam_update(
            params, row_grad, first_moment, second_moment, weight_decay
        )
    gain_terms = jnp.stack([gain_one, gain_two, gain_three, gain_four])
    gain_total = butterfly_sum(
        butterfly_sum(gain_terms, WIDE, wide_count), "shard", shard_count
    )
    gain_grad = lax.dynamic_slice_in_dim(
        gain_total, lax.axis_index("shard") * gains.shape[1], gains.shape[1], axis=1
    )
    new_gains, new_gain_first, new_gain_second = adam_update(
        gains, gain_grad, gain_first, gain_second, 0.0
    )
    return (
        result.astype(jnp.bfloat16),
        input_grad.astype(jnp.bfloat16),
        row_grad,
        gain_grad,
        new_params,
        new_gains,
        new_first,
        new_second,
        new_gain_first,
        new_gain_second,
    )


def solution(mesh):
    wide = mesh.shape["wide"]

    split_mesh = Mesh(
        mesh.devices.reshape(wide // 2, 2, mesh.shape["shard"]),
        ("chip", "core", "shard"),
    )
    return jax.shard_map(
        per_device,
        mesh=split_mesh,
        in_specs=(
            P(("chip", "core", "shard"), None),
            P(("chip", "core", "shard")),
            P(("chip", "core", "shard"), None),
            P("shard", None),
            P(None, "shard"),
            P("shard", None),
            P("shard", None),
            P(None, "shard"),
            P(None, "shard"),
        ),
        out_specs=(
            P(("chip", "core", "shard"), None),
            P(("chip", "core", "shard"), None),
            P("shard", None),
            P(None, "shard"),
            P("shard", None),
            P(None, "shard"),
            P("shard", None),
            P("shard", None),
            P(None, "shard"),
            P(None, "shard"),
        ),
        check_vma=False,
    )
```

```python
import jax
import jax.numpy as jnp
from jax import lax
from jax.experimental import pallas as pl
from jax.experimental.pallas import tpu as pltpu
from jax.sharding import Mesh
from jax.sharding import PartitionSpec as P


D = 1152
FF = 6912
HEADS = 4
KV_HEADS = 1
HD = 256
WINDOW = 512


norm_epsilon = 1e-06
softcap_limit = 50.0
rope_base = 10000.0
beta_first = 0.9
beta_second = 0.95
learn_rate = 0.02
adam_epsilon = 1e-08
weight_decay = 0.1
adam_step = 10.0
masked_floor = -1e30


def rms_scale(values, gain_row):
    return (
        values
        * lax.rsqrt(jnp.mean(values * values, axis=-1, keepdims=True) + norm_epsilon)
        * (1.0 + gain_row)
    )


def positions_of(segments):
    index_row = jnp.arange(segments.shape[0], dtype=jnp.int32)
    previous = jnp.concatenate([segments[:1] - 1, segments[:-1]])
    first_slot = lax.cummax(jnp.where(segments != previous, index_row, 0), axis=0)
    return index_row - first_slot


def rotary_tables(positions, head_width):
    half_width = head_width // 2
    frequency = rope_base ** (-2.0 * jnp.arange(half_width, dtype=jnp.float32) / head_width)
    angles = positions.astype(jnp.float32)[:, None] * frequency[None, :]
    return (jnp.cos(angles), jnp.sin(angles))


def rotate(values, cosine_table, sine_table):
    half_width = values.shape[-1] // 2
    first_half = values[..., :half_width]
    second_half = values[..., half_width:]
    cosine_part = cosine_table[:, None, :]
    sine_part = sine_table[:, None, :]
    return jnp.concatenate(
        [
            first_half * cosine_part - second_half * sine_part,
            second_half * cosine_part + first_half * sine_part,
        ],
        axis=-1,
    )


def contract_rows(left_side, right_side):
    return lax.dot_general(
        left_side, right_side, (((0,), (0,)), ((), ())), preferred_element_type=jnp.float32
    )


def times_transposed(left_side, right_side):
    return lax.dot_general(
        left_side, right_side, (((1,), (1,)), ((), ())), preferred_element_type=jnp.float32
    )


def block_mask(query_segments, key_segments, first_row):
    query_index = first_row + jnp.arange(query_segments.shape[0], dtype=jnp.int32)
    key_index = jnp.arange(key_segments.shape[0], dtype=jnp.int32)
    return (
        (query_segments[:, None] == key_segments[None, :])
        & (key_index[None, :] <= query_index[:, None])
        & (query_index[:, None] - key_index[None, :] < WINDOW)
    )


def adam_update(param_old, grad_sum, first_old, second_old, decay_rate):
    first_new = beta_first * first_old + (1.0 - beta_first) * grad_sum
    second_new = beta_second * second_old + (1.0 - beta_second) * grad_sum * grad_sum
    corrected = (
        first_new
        / (1.0 - beta_first**adam_step)
        / (jnp.sqrt(second_new / (1.0 - beta_second**adam_step)) + adam_epsilon)
    )
    return (param_old - learn_rate * (corrected + decay_rate * param_old), first_new, second_new)


def power_of_two(count):
    return count & (count - 1) == 0


WIDE = ("chip", "core")


def wide_size():
    return lax.axis_size("chip") * lax.axis_size("core")


def butterfly_sum(values, axis_name, count):
    if not power_of_two(count):
        return lax.psum(values, axis_name)
    step = 1
    while step < count:
        values = values + lax.ppermute(values, axis_name, [(i, i ^ step) for i in range(count)])
        step *= 2
    return values


def gather_columns(values, axis_name):
    count = lax.axis_size(axis_name)
    index = lax.axis_index(axis_name)
    width = values.shape[1]
    whole = jnp.zeros((values.shape[0], width * count), values.dtype)
    whole = lax.dynamic_update_slice_in_dim(whole, values, index * width, axis=1)
    for shift in range(1, count):
        moved = lax.ppermute(values, axis_name, [(i, (i + shift) % count) for i in range(count)])
        source = lax.rem(index + count - shift, count)
        whole = lax.dynamic_update_slice_in_dim(whole, moved, source * width, axis=1)
    return whole


def spread_first(rows):
    place = lax.axis_index("shard")
    far = lax.ppermute(rows, "shard", [(0, 2)])
    rows = jnp.where(place == 0, rows, far)
    near = lax.ppermute(rows, "shard", [(0, 1), (2, 3)])
    rows = jnp.where(lax.rem(place, 2) == 1, near, rows)
    index = lax.axis_index(WIDE)
    blocks = {0: rows}
    for bit in (4, 2, 1):
        upper = (index & bit) != 0
        grown = {}
        for key, block in blocks.items():
            other = lax.ppermute(block, WIDE, [(i, i ^ bit) for i in range(8)])
            grown[key] = jnp.where(upper, other, block)
            grown[key | bit] = jnp.where(upper, block, other)
        blocks = grown
    return jnp.concatenate([blocks[key] for key in range(8)], axis=0)


owner_tree = {
    0: ([(3, 2), (1, 0)], [(2, 0)]),
    1: ([(0, 1), (3, 2)], [(2, 1)]),
    2: ([(3, 2), (0, 1)], [(1, 2)]),
    3: ([(0, 1), (2, 3)], [(1, 3)]),
}


def add_low(left, right):
    return (left.astype(jnp.float32) + right.astype(jnp.float32)).astype(left.dtype)


def tied(anchor, values):
    return lax.optimization_barrier((anchor, values))


def choose_owner(pieces):
    place = lax.axis_index("shard")
    own = pieces[0]
    for owner in range(1, len(pieces)):
        own = jnp.where(place == owner, pieces[owner], own)
    return own


def to_partner(values):
    return lax.ppermute(values, "core", [(0, 1), (1, 0)])


def paired(values):
    return jnp.concatenate([values, to_partner(values)], axis=0)


def split_rows(rows):
    return rows.reshape(rows.shape[0] // 16, 2, 8, rows.shape[1])


def one_parity(rows, parity):
    grouped = split_rows(rows)
    return lax.dynamic_index_in_dim(grouped, parity, axis=1, keepdims=False).reshape(
        rows.shape[0] // 2, rows.shape[1]
    )


ends_apart = [(0, 1), (1, 0), (2, 3), (3, 2)]
middle_pair = [(1, 2), (2, 1)]
outward = [(1, 0), (2, 3)]


def gather_rows(params, parity):
    count = params.shape[0] // 2
    place = lax.axis_index("shard")
    middle = (place == 1) | (place == 2)
    part = 2 * count // lax.axis_size("chip")
    piece = one_parity(
        lax.dynamic_slice_in_dim(params, lax.axis_index("chip") * part, part, axis=0), parity
    ).astype(jnp.bfloat16)

    def moved(values, pairs):
        return lax.ppermute(values, "shard", pairs)

    near = moved(piece, ends_apart)
    inner = moved(piece, middle_pair)
    crossed = moved(near, middle_pair)
    second = jnp.where(middle, inner, moved(inner, outward))
    third = jnp.where(middle, crossed, moved(crossed, outward))
    upper = place >= 2
    owners = (
        jnp.where(place % 2 == 0, place + 1, place - 1),
        jnp.where(upper, 1, 2),
        jnp.where(upper, 0, 3),
    )
    own = one_parity(lax.optimization_barrier(params), parity).astype(jnp.bfloat16)
    whole = lax.dynamic_update_slice_in_dim(
        jnp.zeros((4 * count, D), jnp.bfloat16), own, place * count, axis=0
    )
    for owner, rows in zip(owners, (near, second, third)):
        rows = lax.all_gather(rows, "chip", axis=0, tiled=True)
        whole = lax.dynamic_update_slice_in_dim(whole, rows, owner * count, axis=0)
    return whole


def adam_rows(place, block, grad_low, state, carried):
    groups = block // 8

    def rows_of(i, place_ref):
        return (place_ref[0] + (i // 2) * place_ref[1], i % 2, 0, 0)

    spec = pl.BlockSpec((pl.Element(groups), pl.Element(1), pl.Element(8), pl.Element(D)), rows_of)

    def body(place_ref, grad_ref, param_ref, first_ref, second_ref, *rest):
        out_refs = rest[-4:]
        grad = grad_ref[...].astype(jnp.float32).reshape(groups, 1, 8, D)
        param_new, first_new, second_new = adam_update(
            param_ref[...], grad, first_ref[...], second_ref[...], weight_decay
        )
        for ref, value in zip(out_refs, (grad, param_new, first_new, second_new)):
            ref[...] = value

    count = grad_low.shape[0]
    shape = jax.ShapeDtypeStruct(state[0].shape, jnp.float32)
    return pl.pallas_call(
        body,
        grid_spec=pltpu.PrefetchScalarGridSpec(
            num_scalar_prefetch=1,
            grid=(count // block,),
            in_specs=[pl.BlockSpec((block, D), lambda i, place_ref: (i, 0))]
            + [spec] * 3
            + [pl.BlockSpec(memory_space=pl.ANY)] * len(carried),
            out_specs=[spec] * 4,
        ),
        out_shape=[shape] * 4,
        input_output_aliases={5 + k: k for k in range(len(carried))},
        cost_estimate=pl.CostEstimate(
            flops=20 * count * D, transcendentals=count * D, bytes_accessed=30 * count * D
        ),
        compiler_params=pltpu.CompilerParams(vmem_limit_bytes=56 * 2**20),
        name="adam_rows",
    )(place, grad_low, *state, *carried)


def per_device(
    tokens, seg_ids, cotangent, params, gains, first_moment, second_moment, gain_first, gain_second
):
    wide_count = wide_size()
    shard_count = lax.axis_size("shard")
    tree = wide_count == 8 and shard_count == 4
    owner_rows = params.shape[0]
    total_rows = owner_rows * shard_count
    early_rows = (HEADS + 2 * KV_HEADS) * HD + HEADS * HD
    wide_index = lax.axis_index(WIDE)
    core_index = lax.axis_index("core")

    def own_slice(first, count):
        part = count // wide_count
        return lax.dynamic_slice_in_dim(
            params, first + wide_index * part, part, axis=0
        ).astype(jnp.bfloat16)

    if tree:
        rows_used = gather_rows(params, core_index)
        early_used = spread_first(own_slice(0, early_rows))
        split = 2
    else:
        rows_used = lax.all_gather(
            own_slice(0, owner_rows), ("shard",) + WIDE, axis=0, tiled=True
        )
        early_used = rows_used[:early_rows]
        split = 1
    gains_used = gather_columns(gains.astype(jnp.bfloat16), "shard")
    gains_float = gains_used.astype(jnp.float32)
    query_width = HEADS * HD
    kv_width = KV_HEADS * HD
    per_group = HEADS // KV_HEADS
    qkv_rows = query_width + 2 * kv_width
    out_end = qkv_rows + query_width
    gate_end = out_end + 2 * FF
    w_qkv = early_used[:qkv_rows]
    w_out = early_used[qkv_rows:out_end]
    gate_first, up_first, down_first, hidden_width = (
        out_end // split,
        (out_end + FF) // split,
        gate_end // split,
        FF // split,
    )
    w_gate_up = rows_used[gate_first:down_first]
    w_down = rows_used[down_first:]
    row_count = tokens.shape[0]
    block_rows = min(512, row_count)
    block_count = row_count // block_rows
    query_scale = HD ** (-0.5)
    inputs = tokens.astype(jnp.float32)
    cosine_table, sine_table = rotary_tables(positions_of(seg_ids), HD)
    normed, pull_first = jax.vjp(rms_scale, inputs, gains_float[0])
    normed_low = normed.astype(jnp.bfloat16)
    projected = times_transposed(normed_low, w_qkv)
    query_raw = projected[:, :query_width].reshape(row_count, HEADS, HD)
    key_raw = projected[:, query_width : query_width + kv_width].reshape(row_count, KV_HEADS, HD)
    value_heads = (
        projected[:, query_width + kv_width :].astype(jnp.bfloat16).reshape(row_count, KV_HEADS, HD)
    )
    queries = (rotate(query_raw, cosine_table, sine_table) * query_scale).astype(jnp.bfloat16)
    key_heads = rotate(key_raw, cosine_table, sine_table).astype(jnp.bfloat16)
    query_blocks = queries.reshape(block_count, block_rows, KV_HEADS, per_group, HD)
    segment_blocks = seg_ids.reshape(block_count, block_rows)
    block_starts = jnp.arange(block_count, dtype=jnp.int32) * block_rows

    def forward_block(inputs_block):
        query_block, segment_block, first_row = inputs_block
        scores = jnp.einsum(
            "qgnd,kgd->gnqk", query_block, key_heads, preferred_element_type=jnp.float32
        )
        capped = softcap_limit * jnp.tanh(scores / softcap_limit)
        allowed = block_mask(segment_block, seg_ids, first_row)
        row_top = jnp.max(jnp.where(allowed, capped, masked_floor), axis=-1, keepdims=True)
        weights_exp = jnp.where(allowed, jnp.exp(jnp.where(allowed, capped - row_top, 0.0)), 0.0)
        totals = jnp.sum(weights_exp, axis=-1, keepdims=True)
        probability = (weights_exp / totals).astype(jnp.bfloat16)
        mixed_block = jnp.einsum(
            "gnqk,kgd->qgnd", probability, value_heads, preferred_element_type=jnp.float32
        )
        return (mixed_block, row_top + jnp.log(totals))

    mixed_heads, log_totals = lax.map(forward_block, (query_blocks, segment_blocks, block_starts))
    mixed_low = mixed_heads.reshape(row_count, query_width).astype(jnp.bfloat16)
    attended = jnp.dot(mixed_low, w_out, preferred_element_type=jnp.float32)
    attn_normed, pull_second = jax.vjp(rms_scale, attended, gains_float[1])
    first_sum = inputs + attn_normed
    ffn_input, pull_third = jax.vjp(rms_scale, first_sum, gains_float[2])
    ffn_low = ffn_input.astype(jnp.bfloat16)
    if tree:
        ffn_low = paired(ffn_low)
    gate_up_kept = lax.optimization_barrier(
        times_transposed(ffn_low, w_gate_up).astype(jnp.bfloat16)
    )

    gate = gate_up_kept[:, :hidden_width].astype(jnp.float32)
    up = gate_up_kept[:, hidden_width:].astype(jnp.float32)
    active, pull_active = jax.vjp(lambda v: jax.nn.gelu(v, approximate=True), gate)
    gate_factor = (pull_active(jnp.ones_like(gate))[0] * up).astype(jnp.bfloat16)
    hidden = active * up
    hidden_low, gate_factor, up_factor = lax.optimization_barrier(
        (hidden.astype(jnp.bfloat16), gate_factor, active.astype(jnp.bfloat16))
    )
    if tree:
        other_branch = jnp.dot(
            hidden_low[row_count:], w_down, preferred_element_type=jnp.float32
        )
        hidden_low, other_branch = tied(hidden_low, other_branch)
        own_branch, other_branch = tied(
            jnp.dot(hidden_low[:row_count], w_down, preferred_element_type=jnp.float32),
            to_partner(other_branch),
        )
        branch = own_branch + other_branch
    else:
        branch = jnp.dot(hidden_low, w_down, preferred_element_type=jnp.float32)
    ffn_normed, pull_fifth = jax.vjp(rms_scale, branch, gains_float[3])
    result = first_sum + ffn_normed
    upstream = cotangent.astype(jnp.float32)
    branch_grad, gain_four = pull_fifth(upstream)
    branch_low = branch_grad.astype(jnp.bfloat16)
    if tree:
        branch_low = paired(branch_low)

    def product_rows(left, right):
        def rows(first, last):
            return contract_rows(left[:, first:last], right).astype(jnp.bfloat16)

        return rows

    factors = {
        "down": (down_first, total_rows // split, product_rows(hidden_low, branch_low))
    }
    steps = {}
    late_rows = early_rows // split
    segment_rows = owner_rows // split

    def bounds(key):
        return (max(key * segment_rows, late_rows), (key + 1) * segment_rows)

    def plane_terms(first, last):
        parts = [
            rows(max(first, start) - start, min(last, end) - start)
            for start, end, rows in sorted(factors.values(), key=lambda f: f[0])
            if max(first, start) < min(last, end)
        ]
        return parts[0] if len(parts) == 1 else jnp.concatenate(parts, axis=0)

    def start_ready(anchor, lowest):
        keys = [
            key
            for key in reversed(range(shard_count))
            if key not in steps and bounds(key)[0] >= lowest
        ]
        if not tree or not keys:
            return anchor
        terms = [plane_terms(*bounds(key)) for key in keys]
        for key, term in zip(keys, terms):
            steps[key] = [lax.psum_scatter(term, "chip", scatter_dimension=0, tiled=True)]
        return tied(anchor, terms)[0]

    def advance(key):
        pairs = owner_tree[max(key, 0)][len(steps[key]) - 1]
        held = steps[key][-1]
        moved = lax.ppermute(held, "shard", pairs)
        steps[key].append(add_low(held, moved))

    def tick(anchor, *keys):
        if not tree:
            return anchor
        anchor, values = tied(anchor, [steps[key][-1] for key in keys])
        for key, value in zip(keys, values):
            steps[key][-1] = value
            advance(key)
        return anchor

    branch_low = start_ready(branch_low, down_first)
    hidden_grad = times_transposed(branch_low, w_down)
    gate_grad = hidden_grad * gate_factor.astype(jnp.float32)
    up_grad = hidden_grad * up_factor.astype(jnp.float32)
    gate_low, up_low = gate_grad.astype(jnp.bfloat16), up_grad.astype(jnp.bfloat16)
    factors["gate"] = (gate_first, up_first, product_rows(gate_low, ffn_low))
    factors["up"] = (up_first, down_first, product_rows(up_low, ffn_low))
    gate_low, up_low = start_ready((gate_low, up_low), gate_first)
    gate_low, up_low = tick((gate_low, up_low), 3)

    def input_grad_of(first, last):
        return jnp.dot(
            gate_low[first:last], w_gate_up[:hidden_width], preferred_element_type=jnp.float32
        ) + jnp.dot(
            up_low[first:last], w_gate_up[hidden_width:], preferred_element_type=jnp.float32
        )

    if tree:
        other_grad = input_grad_of(row_count, 2 * row_count)
        (gate_low, up_low), other_grad = tied((gate_low, up_low), other_grad)
        ffn_input_grad = input_grad_of(0, row_count) + to_partner(other_grad)
    else:
        ffn_input_grad = input_grad_of(0, row_count)
    ffn_input_grad = tick(ffn_input_grad, 2)
    sum_grad_part, gain_three = pull_third(ffn_input_grad)
    sum_grad = upstream + sum_grad_part
    attended_grad, gain_two = pull_second(sum_grad)
    attended_low = attended_grad.astype(jnp.bfloat16)
    out_rows = product_rows(mixed_low, attended_low)

    factors["out"] = (qkv_rows // split, gate_first, out_rows)

    mixed_grad = (
        times_transposed(attended_low, w_out)
        .astype(jnp.bfloat16)
        .reshape(block_count, block_rows, KV_HEADS, per_group, HD)
    )

    mixed_grad = start_ready(mixed_grad, late_rows)
    mixed_grad = tick(mixed_grad, 3)

    def backward_block(running, inputs_block):
        key_acc, value_acc = running
        query_block, grad_block, segment_block, first_row, log_block = inputs_block
        scores = jnp.einsum(
            "qgnd,kgd->gnqk", query_block, key_heads, preferred_element_type=jnp.float32
        )
        capped = softcap_limit * jnp.tanh(scores / softcap_limit)
        allowed = block_mask(segment_block, seg_ids, first_row)
        probability = jnp.where(allowed, jnp.exp(jnp.where(allowed, capped - log_block, 0.0)), 0.0)
        probability_low = probability.astype(jnp.bfloat16)
        value_acc = value_acc + jnp.einsum(
            "gnqk,qgnd->kgd", probability_low, grad_block, preferred_element_type=jnp.float32
        )
        prob_grad = jnp.einsum(
            "qgnd,kgd->gnqk", grad_block, value_heads, preferred_element_type=jnp.float32
        )
        centred = jnp.sum(probability * prob_grad, axis=-1, keepdims=True)
        score_grad = (
            probability * (prob_grad - centred) * (1.0 - (capped / softcap_limit) ** 2)
        ).astype(jnp.bfloat16)
        query_grad_block = jnp.einsum(
            "gnqk,kgd->qgnd", score_grad, key_heads, preferred_element_type=jnp.float32
        )
        key_acc = key_acc + jnp.einsum(
            "gnqk,qgnd->kgd", score_grad, query_block, preferred_element_type=jnp.float32
        )
        return ((key_acc, value_acc), query_grad_block)

    zero_heads = jnp.zeros((row_count, KV_HEADS, HD), jnp.float32)
    (key_grad, value_grad), query_grad = lax.scan(
        backward_block,
        (zero_heads, zero_heads),
        (query_blocks, mixed_grad, segment_blocks, block_starts, log_totals),
    )
    query_grad = tick(query_grad, 2, 1)
    query_raw_grad = rotate(
        query_grad.reshape(row_count, HEADS, HD) * query_scale, cosine_table, -sine_table
    )
    key_raw_grad = rotate(key_grad, cosine_table, -sine_table)
    qkv_low = jnp.concatenate(
        [
            query_raw_grad.reshape(row_count, query_width),
            key_raw_grad.reshape(row_count, kv_width),
            value_grad.reshape(row_count, kv_width),
        ],
        axis=1,
    ).astype(jnp.bfloat16)
    factors["qkv"] = (0, qkv_rows // split, product_rows(qkv_low, normed_low))
    normed_grad = jnp.dot(qkv_low, w_qkv, preferred_element_type=jnp.float32)
    input_part, gain_one = pull_first(normed_grad)
    input_grad = sum_grad + input_part
    state = (params, first_moment, second_moment)
    if tree:
        qkv_grad = product_rows(qkv_low, normed_low)(0, qkv_rows)
        late_grad = jnp.concatenate([qkv_grad, out_rows(0, query_width)], axis=0)
        by_piece = (
            late_grad.reshape(wide_count // 2, -1, 2, 8, D)
            .transpose(0, 2, 1, 3, 4)
            .reshape(early_rows, D)
        )
        steps[-1] = [lax.psum_scatter(by_piece, WIDE, scatter_dimension=0, tiled=True)]
        for key in (3, 2, 1, 0, -1):
            while len(steps[key]) < 3:
                advance(key)
        late_part = early_rows // wide_count
        early_part = owner_rows // wide_count - late_part
        whole_pieces = [steps[owner][-1] for owner in range(1, shard_count)]
        early_piece = choose_owner([steps[0][-1]] + [p[:early_part] for p in whole_pieces])
        late_piece = choose_owner([steps[-1][-1]] + [p[early_part:] for p in whole_pieces])
        first_owner = lax.axis_index("shard") == 0
        early_groups, late_groups = early_part // 8, late_part // 8
        early_place = jnp.where(
            first_owner,
            jnp.array([early_rows // 16, early_groups], jnp.int32),
            jnp.array([0, early_groups + late_groups], jnp.int32),
        )
        late_place = jnp.where(
            first_owner,
            jnp.array([0, late_groups], jnp.int32),
            jnp.array([early_groups, early_groups + late_groups], jnp.int32),
        )
        early_low = lax.all_gather(early_piece, WIDE, axis=0, tiled=True)
        late_low = lax.all_gather(late_piece, WIDE, axis=0, tiled=True)
        state = [split_rows(rows) for rows in (params, first_moment, second_moment)]
        carried = adam_rows(early_place, early_part, early_low, state, ())
        row_grad, new_params, new_first, new_second = [
            rows.reshape(owner_rows, D)
            for rows in adam_rows(late_place, late_part, late_low, state, carried)
        ]
    else:
        own = lax.psum_scatter(
            plane_terms(0, total_rows), ("shard",) + WIDE, scatter_dimension=0, tiled=True
        )
        row_grad = lax.all_gather(own, WIDE, axis=0, tiled=True).astype(jnp.float32)
        new_params, new_first, new_second = adam_update(
            params, row_grad, first_moment, second_moment, weight_decay
        )
    gain_terms = jnp.stack([gain_one, gain_two, gain_three, gain_four])
    gain_total = butterfly_sum(
        butterfly_sum(gain_terms, WIDE, wide_count), "shard", shard_count
    )
    gain_grad = lax.dynamic_slice_in_dim(
        gain_total, lax.axis_index("shard") * gains.shape[1], gains.shape[1], axis=1
    )
    new_gains, new_gain_first, new_gain_second = adam_update(
        gains, gain_grad, gain_first, gain_second, 0.0
    )
    return (
        result.astype(jnp.bfloat16),
        input_grad.astype(jnp.bfloat16),
        row_grad,
        gain_grad,
        new_params,
        new_gains,
        new_first,
        new_second,
        new_gain_first,
        new_gain_second,
    )


def solution(mesh):
    wide = mesh.shape["wide"]

    split_mesh = Mesh(
        mesh.devices.reshape(wide // 2, 2, mesh.shape["shard"]),
        ("chip", "core", "shard"),
    )
    return jax.shard_map(
        per_device,
        mesh=split_mesh,
        in_specs=(
            P(("chip", "core", "shard"), None),
            P(("chip", "core", "shard")),
            P(("chip", "core", "shard"), None),
            P("shard", None),
            P(None, "shard"),
            P("shard", None),
            P("shard", None),
            P(None, "shard"),
            P(None, "shard"),
        ),
        out_specs=(
            P(("chip", "core", "shard"), None),
            P(("chip", "core", "shard"), None),
            P("shard", None),
            P(None, "shard"),
            P("shard", None),
            P(None, "shard"),
            P("shard", None),
            P("shard", None),
            P(None, "shard"),
            P(None, "shard"),
        ),
        check_vma=False,
    )
```

```python
import jax
import jax.numpy as jnp
from jax import lax
from jax.experimental import pallas as pl
from jax.experimental.pallas import tpu as pltpu
from jax.sharding import Mesh
from jax.sharding import PartitionSpec as P


D = 1152
FF = 6912
HEADS = 4
KV_HEADS = 1
HD = 256
WINDOW = 512


norm_epsilon = 1e-06
softcap_limit = 50.0
rope_base = 10000.0
beta_first = 0.9
beta_second = 0.95
learn_rate = 0.02
adam_epsilon = 1e-08
weight_decay = 0.1
adam_step = 10.0
masked_floor = -1e30


def rms_scale(values, gain_row):
    return (
        values
        * lax.rsqrt(jnp.mean(values * values, axis=-1, keepdims=True) + norm_epsilon)
        * (1.0 + gain_row)
    )


def positions_of(segments):
    index_row = jnp.arange(segments.shape[0], dtype=jnp.int32)
    previous = jnp.concatenate([segments[:1] - 1, segments[:-1]])
    first_slot = lax.cummax(jnp.where(segments != previous, index_row, 0), axis=0)
    return index_row - first_slot


def rotary_tables(positions, head_width):
    half_width = head_width // 2
    frequency = rope_base ** (-2.0 * jnp.arange(half_width, dtype=jnp.float32) / head_width)
    angles = positions.astype(jnp.float32)[:, None] * frequency[None, :]
    return (jnp.cos(angles), jnp.sin(angles))


def rotate(values, cosine_table, sine_table):
    half_width = values.shape[-1] // 2
    first_half = values[..., :half_width]
    second_half = values[..., half_width:]
    cosine_part = cosine_table[:, None, :]
    sine_part = sine_table[:, None, :]
    return jnp.concatenate(
        [
            first_half * cosine_part - second_half * sine_part,
            second_half * cosine_part + first_half * sine_part,
        ],
        axis=-1,
    )


def contract_rows(left_side, right_side):
    return lax.dot_general(
        left_side, right_side, (((0,), (0,)), ((), ())), preferred_element_type=jnp.float32
    )


def times_transposed(left_side, right_side):
    return lax.dot_general(
        left_side, right_side, (((1,), (1,)), ((), ())), preferred_element_type=jnp.float32
    )


def block_mask(query_segments, key_segments, first_row):
    query_index = first_row + jnp.arange(query_segments.shape[0], dtype=jnp.int32)
    key_index = jnp.arange(key_segments.shape[0], dtype=jnp.int32)
    return (
        (query_segments[:, None] == key_segments[None, :])
        & (key_index[None, :] <= query_index[:, None])
        & (query_index[:, None] - key_index[None, :] < WINDOW)
    )


def adam_update(param_old, grad_sum, first_old, second_old, decay_rate):
    first_new = beta_first * first_old + (1.0 - beta_first) * grad_sum
    second_new = beta_second * second_old + (1.0 - beta_second) * grad_sum * grad_sum
    corrected = (
        first_new
        / (1.0 - beta_first**adam_step)
        / (jnp.sqrt(second_new / (1.0 - beta_second**adam_step)) + adam_epsilon)
    )
    return (param_old - learn_rate * (corrected + decay_rate * param_old), first_new, second_new)


def power_of_two(count):
    return count & (count - 1) == 0


WIDE = ("chip", "core")


def wide_size():
    return lax.axis_size("chip") * lax.axis_size("core")


def butterfly_sum(values, axis_name, count):
    if not power_of_two(count):
        return lax.psum(values, axis_name)
    step = 1
    while step < count:
        values = values + lax.ppermute(values, axis_name, [(i, i ^ step) for i in range(count)])
        step *= 2
    return values


def gather_columns(values, axis_name):
    count = lax.axis_size(axis_name)
    index = lax.axis_index(axis_name)
    width = values.shape[1]
    whole = jnp.zeros((values.shape[0], width * count), values.dtype)
    whole = lax.dynamic_update_slice_in_dim(whole, values, index * width, axis=1)
    for shift in range(1, count):
        moved = lax.ppermute(values, axis_name, [(i, (i + shift) % count) for i in range(count)])
        source = lax.rem(index + count - shift, count)
        whole = lax.dynamic_update_slice_in_dim(whole, moved, source * width, axis=1)
    return whole


def spread_first(rows):
    place = lax.axis_index("shard")
    far = lax.ppermute(rows, "shard", [(0, 2)])
    rows = jnp.where(place == 0, rows, far)
    near = lax.ppermute(rows, "shard", [(0, 1), (2, 3)])
    rows = jnp.where(lax.rem(place, 2) == 1, near, rows)
    index = lax.axis_index(WIDE)
    blocks = {0: rows}
    for bit in (4, 2, 1):
        upper = (index & bit) != 0
        grown = {}
        for key, block in blocks.items():
            other = lax.ppermute(block, WIDE, [(i, i ^ bit) for i in range(8)])
            grown[key] = jnp.where(upper, other, block)
            grown[key | bit] = jnp.where(upper, block, other)
        blocks = grown
    return jnp.concatenate([blocks[key] for key in range(8)], axis=0)


owner_tree = {
    0: ([(3, 2), (1, 0)], [(2, 0)]),
    1: ([(0, 1), (3, 2)], [(2, 1)]),
    2: ([(3, 2), (0, 1)], [(1, 2)]),
    3: ([(0, 1), (2, 3)], [(1, 3)]),
}


def add_low(left, right):
    return (left.astype(jnp.float32) + right.astype(jnp.float32)).astype(left.dtype)


def tied(anchor, values):
    return lax.optimization_barrier((anchor, values))


def choose_owner(pieces):
    place = lax.axis_index("shard")
    own = pieces[0]
    for owner in range(1, len(pieces)):
        own = jnp.where(place == owner, pieces[owner], own)
    return own


def to_partner(values):
    return lax.ppermute(values, "core", [(0, 1), (1, 0)])


def paired(values):
    return jnp.concatenate([values, to_partner(values)], axis=0)


def split_rows(rows):
    return rows.reshape(rows.shape[0] // 16, 2, 8, rows.shape[1])


def one_parity(rows, parity):
    grouped = split_rows(rows)
    return lax.dynamic_index_in_dim(grouped, parity, axis=1, keepdims=False).reshape(
        rows.shape[0] // 2, rows.shape[1]
    )


ends_apart = [(0, 1), (1, 0), (2, 3), (3, 2)]
middle_pair = [(1, 2), (2, 1)]
outward = [(1, 0), (2, 3)]


def gather_rows(params, parity):
    count = params.shape[0] // 2
    place = lax.axis_index("shard")
    middle = (place == 1) | (place == 2)
    part = 2 * count // lax.axis_size("chip")
    piece = one_parity(
        lax.dynamic_slice_in_dim(params, lax.axis_index("chip") * part, part, axis=0), parity
    ).astype(jnp.bfloat16)

    def moved(values, pairs):
        return lax.ppermute(values, "shard", pairs)

    near = moved(piece, ends_apart)
    inner = moved(piece, middle_pair)
    crossed = moved(near, middle_pair)
    second = jnp.where(middle, inner, moved(inner, outward))
    third = jnp.where(middle, crossed, moved(crossed, outward))
    upper = place >= 2
    owners = (
        jnp.where(place % 2 == 0, place + 1, place - 1),
        jnp.where(upper, 1, 2),
        jnp.where(upper, 0, 3),
    )
    own = one_parity(lax.optimization_barrier(params), parity).astype(jnp.bfloat16)
    whole = lax.dynamic_update_slice_in_dim(
        jnp.zeros((4 * count, D), jnp.bfloat16), own, place * count, axis=0
    )
    for owner, rows in zip(owners, (near, second, third)):
        rows = lax.all_gather(rows, "chip", axis=0, tiled=True)
        whole = lax.dynamic_update_slice_in_dim(whole, rows, owner * count, axis=0)
    return whole


def adam_rows(place, block, grad_low, state, carried):
    groups = block // 8

    def rows_of(i, place_ref):
        return (place_ref[0] + (i // 2) * place_ref[1], i % 2, 0, 0)

    spec = pl.BlockSpec((pl.Element(groups), pl.Element(1), pl.Element(8), pl.Element(D)), rows_of)

    def body(place_ref, grad_ref, param_ref, first_ref, second_ref, *rest):
        out_refs = rest[-4:]
        grad = grad_ref[...].astype(jnp.float32).reshape(groups, 1, 8, D)
        param_new, first_new, second_new = adam_update(
            param_ref[...], grad, first_ref[...], second_ref[...], weight_decay
        )
        for ref, value in zip(out_refs, (grad, param_new, first_new, second_new)):
            ref[...] = value

    count = grad_low.shape[0]
    shape = jax.ShapeDtypeStruct(state[0].shape, jnp.float32)
    return pl.pallas_call(
        body,
        grid_spec=pltpu.PrefetchScalarGridSpec(
            num_scalar_prefetch=1,
            grid=(count // block,),
            in_specs=[pl.BlockSpec((block, D), lambda i, place_ref: (i, 0))]
            + [spec] * 3
            + [pl.BlockSpec(memory_space=pl.ANY)] * len(carried),
            out_specs=[spec] * 4,
        ),
        out_shape=[shape] * 4,
        input_output_aliases={5 + k: k for k in range(len(carried))},
        cost_estimate=pl.CostEstimate(
            flops=20 * count * D, transcendentals=count * D, bytes_accessed=30 * count * D
        ),
        compiler_params=pltpu.CompilerParams(vmem_limit_bytes=56 * 2**20),
        name="adam_rows",
    )(place, grad_low, *state, *carried)


def per_device(
    tokens, seg_ids, cotangent, params, gains, first_moment, second_moment, gain_first, gain_second
):
    wide_count = wide_size()
    shard_count = lax.axis_size("shard")
    tree = wide_count == 8 and shard_count == 4
    owner_rows = params.shape[0]
    total_rows = owner_rows * shard_count
    early_rows = (HEADS + 2 * KV_HEADS) * HD + HEADS * HD
    wide_index = lax.axis_index(WIDE)
    core_index = lax.axis_index("core")

    def own_slice(first, count):
        part = count // wide_count
        return lax.dynamic_slice_in_dim(
            params, first + wide_index * part, part, axis=0
        ).astype(jnp.bfloat16)

    if tree:
        rows_used = gather_rows(params, core_index)
        early_used = spread_first(own_slice(0, early_rows))
        split = 2
    else:
        rows_used = lax.all_gather(
            own_slice(0, owner_rows), ("shard",) + WIDE, axis=0, tiled=True
        )
        early_used = rows_used[:early_rows]
        split = 1
    gains_used = gather_columns(gains.astype(jnp.bfloat16), "shard")
    gains_float = gains_used.astype(jnp.float32)
    query_width = HEADS * HD
    kv_width = KV_HEADS * HD
    per_group = HEADS // KV_HEADS
    qkv_rows = query_width + 2 * kv_width
    out_end = qkv_rows + query_width
    gate_end = out_end + 2 * FF
    w_qkv = early_used[:qkv_rows]
    w_out = early_used[qkv_rows:out_end]
    gate_first, up_first, down_first, hidden_width = (
        out_end // split,
        (out_end + FF) // split,
        gate_end // split,
        FF // split,
    )
    w_gate_up = rows_used[gate_first:down_first]
    w_down = rows_used[down_first:]
    row_count = tokens.shape[0]
    block_rows = min(512, row_count)
    block_count = row_count // block_rows
    query_scale = HD ** (-0.5)
    inputs = tokens.astype(jnp.float32)
    cosine_table, sine_table = rotary_tables(positions_of(seg_ids), HD)
    normed, pull_first = jax.vjp(rms_scale, inputs, gains_float[0])
    normed_low = normed.astype(jnp.bfloat16)
    projected = times_transposed(normed_low, w_qkv)
    query_raw = projected[:, :query_width].reshape(row_count, HEADS, HD)
    key_raw = projected[:, query_width : query_width + kv_width].reshape(row_count, KV_HEADS, HD)
    value_heads = (
        projected[:, query_width + kv_width :].astype(jnp.bfloat16).reshape(row_count, KV_HEADS, HD)
    )
    queries = (rotate(query_raw, cosine_table, sine_table) * query_scale).astype(jnp.bfloat16)
    key_heads = rotate(key_raw, cosine_table, sine_table).astype(jnp.bfloat16)
    query_blocks = queries.reshape(block_count, block_rows, KV_HEADS, per_group, HD)
    segment_blocks = seg_ids.reshape(block_count, block_rows)
    block_starts = jnp.arange(block_count, dtype=jnp.int32) * block_rows

    def forward_block(inputs_block):
        query_block, segment_block, first_row = inputs_block
        scores = jnp.einsum(
            "qgnd,kgd->gnqk", query_block, key_heads, preferred_element_type=jnp.float32
        )
        capped = softcap_limit * jnp.tanh(scores / softcap_limit)
        allowed = block_mask(segment_block, seg_ids, first_row)
        row_top = jnp.max(jnp.where(allowed, capped, masked_floor), axis=-1, keepdims=True)
        weights_exp = jnp.where(allowed, jnp.exp(jnp.where(allowed, capped - row_top, 0.0)), 0.0)
        totals = jnp.sum(weights_exp, axis=-1, keepdims=True)
        probability = (weights_exp / totals).astype(jnp.bfloat16)
        mixed_block = jnp.einsum(
            "gnqk,kgd->qgnd", probability, value_heads, preferred_element_type=jnp.float32
        )
        return (mixed_block, row_top + jnp.log(totals))

    mixed_heads, log_totals = lax.map(forward_block, (query_blocks, segment_blocks, block_starts))
    mixed_low = mixed_heads.reshape(row_count, query_width).astype(jnp.bfloat16)
    attended = jnp.dot(mixed_low, w_out, preferred_element_type=jnp.float32)
    attn_normed, pull_second = jax.vjp(rms_scale, attended, gains_float[1])
    first_sum = inputs + attn_normed
    ffn_input, pull_third = jax.vjp(rms_scale, first_sum, gains_float[2])
    ffn_low = ffn_input.astype(jnp.bfloat16)
    if tree:
        ffn_low = paired(ffn_low)
    gate_up_kept = lax.optimization_barrier(
        times_transposed(ffn_low, w_gate_up).astype(jnp.bfloat16)
    )

    gate = gate_up_kept[:, :hidden_width].astype(jnp.float32)
    up = gate_up_kept[:, hidden_width:].astype(jnp.float32)
    active, pull_active = jax.vjp(lambda v: jax.nn.gelu(v, approximate=True), gate)
    gate_factor = (pull_active(jnp.ones_like(gate))[0] * up).astype(jnp.bfloat16)
    hidden = active * up
    hidden_low, gate_factor, up_factor = lax.optimization_barrier(
        (hidden.astype(jnp.bfloat16), gate_factor, active.astype(jnp.bfloat16))
    )
    if tree:
        other_branch = jnp.dot(
            hidden_low[row_count:], w_down, preferred_element_type=jnp.float32
        )
        hidden_low, other_branch = tied(hidden_low, other_branch)
        own_branch, other_branch = tied(
            jnp.dot(hidden_low[:row_count], w_down, preferred_element_type=jnp.float32),
            to_partner(other_branch),
        )
        branch = own_branch + other_branch
    else:
        branch = jnp.dot(hidden_low, w_down, preferred_element_type=jnp.float32)
    ffn_normed, pull_fifth = jax.vjp(rms_scale, branch, gains_float[3])
    result = first_sum + ffn_normed
    upstream = cotangent.astype(jnp.float32)
    branch_grad, gain_four = pull_fifth(upstream)
    branch_low = branch_grad.astype(jnp.bfloat16)
    if tree:
        branch_low = paired(branch_low)

    def product_rows(left, right):
        def rows(first, last):
            return contract_rows(left[:, first:last], right).astype(jnp.bfloat16)

        return rows

    factors = {
        "down": (down_first, total_rows // split, product_rows(hidden_low, branch_low))
    }
    steps = {}
    late_rows = qkv_rows // split
    segment_rows = owner_rows // split

    def bounds(key):
        return (max(key * segment_rows, late_rows), (key + 1) * segment_rows)

    def plane_terms(first, last):
        parts = [
            rows(max(first, start) - start, min(last, end) - start)
            for start, end, rows in sorted(factors.values(), key=lambda f: f[0])
            if max(first, start) < min(last, end)
        ]
        return parts[0] if len(parts) == 1 else jnp.concatenate(parts, axis=0)

    def start_ready(anchor, lowest):
        keys = [
            key
            for key in reversed(range(shard_count))
            if key not in steps and bounds(key)[0] >= lowest
        ]
        if not tree or not keys:
            return anchor
        terms = [plane_terms(*bounds(key)) for key in keys]
        for key, term in zip(keys, terms):
            steps[key] = [lax.psum_scatter(term, "chip", scatter_dimension=0, tiled=True)]
        return tied(anchor, terms)[0]

    def advance(key):
        pairs = owner_tree[max(key, 0)][len(steps[key]) - 1]
        held = steps[key][-1]
        moved = lax.ppermute(held, "shard", pairs)
        steps[key].append(add_low(held, moved))

    def tick(anchor, *keys):
        if not tree:
            return anchor
        anchor, values = tied(anchor, [steps[key][-1] for key in keys])
        for key, value in zip(keys, values):
            steps[key][-1] = value
            advance(key)
        return anchor

    branch_low = start_ready(branch_low, down_first)
    hidden_grad = times_transposed(branch_low, w_down)
    gate_grad = hidden_grad * gate_factor.astype(jnp.float32)
    up_grad = hidden_grad * up_factor.astype(jnp.float32)
    gate_low, up_low = gate_grad.astype(jnp.bfloat16), up_grad.astype(jnp.bfloat16)
    factors["gate"] = (gate_first, up_first, product_rows(gate_low, ffn_low))
    factors["up"] = (up_first, down_first, product_rows(up_low, ffn_low))
    gate_low, up_low = start_ready((gate_low, up_low), gate_first)
    gate_low, up_low = tick((gate_low, up_low), 3)

    def input_grad_of(first, last):
        return jnp.dot(
            gate_low[first:last], w_gate_up[:hidden_width], preferred_element_type=jnp.float32
        ) + jnp.dot(
            up_low[first:last], w_gate_up[hidden_width:], preferred_element_type=jnp.float32
        )

    if tree:
        other_grad = input_grad_of(row_count, 2 * row_count)
        (gate_low, up_low), other_grad = tied((gate_low, up_low), other_grad)
        ffn_input_grad = input_grad_of(0, row_count) + to_partner(other_grad)
    else:
        ffn_input_grad = input_grad_of(0, row_count)
    ffn_input_grad = tick(ffn_input_grad, 2)
    sum_grad_part, gain_three = pull_third(ffn_input_grad)
    sum_grad = upstream + sum_grad_part
    attended_grad, gain_two = pull_second(sum_grad)
    attended_low = attended_grad.astype(jnp.bfloat16)
    out_rows = product_rows(mixed_low, attended_low)

    def summed_out_rows(first, last):
        rows = out_rows(first * 2, last * 2)
        other = to_partner(one_parity(rows, 1 - core_index))
        return add_low(one_parity(rows, core_index), other)

    factors["out"] = (
        qkv_rows // split,
        gate_first,
        summed_out_rows if tree else out_rows,
    )
    mixed_grad = (
        times_transposed(attended_low, w_out)
        .astype(jnp.bfloat16)
        .reshape(block_count, block_rows, KV_HEADS, per_group, HD)
    )

    mixed_grad = start_ready(mixed_grad, late_rows)
    mixed_grad = tick(mixed_grad, 3)

    def backward_block(running, inputs_block):
        key_acc, value_acc = running
        query_block, grad_block, segment_block, first_row, log_block = inputs_block
        scores = jnp.einsum(
            "qgnd,kgd->gnqk", query_block, key_heads, preferred_element_type=jnp.float32
        )
        capped = softcap_limit * jnp.tanh(scores / softcap_limit)
        allowed = block_mask(segment_block, seg_ids, first_row)
        probability = jnp.where(allowed, jnp.exp(jnp.where(allowed, capped - log_block, 0.0)), 0.0)
        probability_low = probability.astype(jnp.bfloat16)
        value_acc = value_acc + jnp.einsum(
            "gnqk,qgnd->kgd", probability_low, grad_block, preferred_element_type=jnp.float32
        )
        prob_grad = jnp.einsum(
            "qgnd,kgd->gnqk", grad_block, value_heads, preferred_element_type=jnp.float32
        )
        centred = jnp.sum(probability * prob_grad, axis=-1, keepdims=True)
        score_grad = (
            probability * (prob_grad - centred) * (1.0 - (capped / softcap_limit) ** 2)
        ).astype(jnp.bfloat16)
        query_grad_block = jnp.einsum(
            "gnqk,kgd->qgnd", score_grad, key_heads, preferred_element_type=jnp.float32
        )
        key_acc = key_acc + jnp.einsum(
            "gnqk,qgnd->kgd", score_grad, query_block, preferred_element_type=jnp.float32
        )
        return ((key_acc, value_acc), query_grad_block)

    zero_heads = jnp.zeros((row_count, KV_HEADS, HD), jnp.float32)
    (key_grad, value_grad), query_grad = lax.scan(
        backward_block,
        (zero_heads, zero_heads),
        (query_blocks, mixed_grad, segment_blocks, block_starts, log_totals),
    )
    query_grad = tick(query_grad, 2, 1)
    query_raw_grad = rotate(
        query_grad.reshape(row_count, HEADS, HD) * query_scale, cosine_table, -sine_table
    )
    key_raw_grad = rotate(key_grad, cosine_table, -sine_table)
    qkv_low = jnp.concatenate(
        [
            query_raw_grad.reshape(row_count, query_width),
            key_raw_grad.reshape(row_count, kv_width),
            value_grad.reshape(row_count, kv_width),
        ],
        axis=1,
    ).astype(jnp.bfloat16)
    factors["qkv"] = (0, qkv_rows // split, product_rows(qkv_low, normed_low))
    normed_grad = jnp.dot(qkv_low, w_qkv, preferred_element_type=jnp.float32)
    input_part, gain_one = pull_first(normed_grad)
    input_grad = sum_grad + input_part
    state = (params, first_moment, second_moment)
    if tree:
        qkv_grad = product_rows(qkv_low, normed_low)(0, qkv_rows)
        by_piece = (
            qkv_grad.reshape(wide_count // 2, -1, 2, 8, D)
            .transpose(0, 2, 1, 3, 4)
            .reshape(qkv_rows, D)
        )
        steps[-1] = [lax.psum_scatter(by_piece, WIDE, scatter_dimension=0, tiled=True)]
        for key in (3, 2, 1, 0, -1):
            while len(steps[key]) < 3:
                advance(key)
        late_part = qkv_rows // wide_count
        early_part = owner_rows // wide_count - late_part
        whole_pieces = [steps[owner][-1] for owner in range(1, shard_count)]
        early_piece = choose_owner([steps[0][-1]] + [p[:early_part] for p in whole_pieces])
        late_piece = choose_owner([steps[-1][-1]] + [p[early_part:] for p in whole_pieces])
        first_owner = lax.axis_index("shard") == 0
        early_groups, late_groups = early_part // 8, late_part // 8
        early_place = jnp.where(
            first_owner,
            jnp.array([qkv_rows // 16, early_groups], jnp.int32),
            jnp.array([0, early_groups + late_groups], jnp.int32),
        )
        late_place = jnp.where(
            first_owner,
            jnp.array([0, late_groups], jnp.int32),
            jnp.array([early_groups, early_groups + late_groups], jnp.int32),
        )
        early_low = lax.all_gather(early_piece, WIDE, axis=0, tiled=True)
        late_low = lax.all_gather(late_piece, WIDE, axis=0, tiled=True)
        state = [split_rows(rows) for rows in (params, first_moment, second_moment)]
        carried = adam_rows(early_place, early_part, early_low, state, ())
        row_grad, new_params, new_first, new_second = [
            rows.reshape(owner_rows, D)
            for rows in adam_rows(late_place, late_part, late_low, state, carried)
        ]
    else:
        own = lax.psum_scatter(
            plane_terms(0, total_rows), ("shard",) + WIDE, scatter_dimension=0, tiled=True
        )
        row_grad = lax.all_gather(own, WIDE, axis=0, tiled=True).astype(jnp.float32)
        new_params, new_first, new_second = adam_update(
            params, row_grad, first_moment, second_moment, weight_decay
        )
    gain_terms = jnp.stack([gain_one, gain_two, gain_three, gain_four])
    gain_total = butterfly_sum(
        butterfly_sum(gain_terms, WIDE, wide_count), "shard", shard_count
    )
    gain_grad = lax.dynamic_slice_in_dim(
        gain_total, lax.axis_index("shard") * gains.shape[1], gains.shape[1], axis=1
    )
    new_gains, new_gain_first, new_gain_second = adam_update(
        gains, gain_grad, gain_first, gain_second, 0.0
    )
    return (
        result.astype(jnp.bfloat16),
        input_grad.astype(jnp.bfloat16),
        row_grad,
        gain_grad,
        new_params,
        new_gains,
        new_first,
        new_second,
        new_gain_first,
        new_gain_second,
    )


def solution(mesh):
    wide = mesh.shape["wide"]

    split_mesh = Mesh(
        mesh.devices.reshape(wide // 2, 2, mesh.shape["shard"]),
        ("chip", "core", "shard"),
    )
    return jax.shard_map(
        per_device,
        mesh=split_mesh,
        in_specs=(
            P(("chip", "core", "shard"), None),
            P(("chip", "core", "shard")),
            P(("chip", "core", "shard"), None),
            P("shard", None),
            P(None, "shard"),
            P("shard", None),
            P("shard", None),
            P(None, "shard"),
            P(None, "shard"),
        ),
        out_specs=(
            P(("chip", "core", "shard"), None),
            P(("chip", "core", "shard"), None),
            P("shard", None),
            P(None, "shard"),
            P("shard", None),
            P(None, "shard"),
            P("shard", None),
            P("shard", None),
            P(None, "shard"),
            P(None, "shard"),
        ),
        check_vma=False,
    )
```
